256 devices in a mesh: pipe: 8 (over x, y_hi), dp: 32 (over y_lo, z, core).
Axes of the slice: x: 4, y: 4 (y_hi: 2, y_lo: 2; y = y_hi * 2 + y_lo), z: 8, core: 2. Of those that a mesh axis runs over, the one named last changes fastest.
Arguments:
- tokens: bfloat16 [2, 64, 32, 4096], P(None, 'dp'), may hold values from -6 to 6
- cotangents: bfloat16 [2, 64, 32, 4096], P(None, 'dp'), may hold values from -1.5 to 1.5
- starts: int32 [2, 64, 4], P(None, 'dp'), may hold values from 0 to 31, as said below
- counts: int32 [2, 64], P(None, 'dp'), may hold values from 1 to 4
- layer_gains: bfloat16 [8, 4096], P('pipe', 'dp'), may hold values from 0.5 to 1.5
- first_map: bfloat16 [8, 4096, 128], P('pipe', 'dp'), may hold values from -0.09375 to 0.09375
- second_map: bfloat16 [8, 128, 4096], P('pipe', None, 'dp'), may hold values from -0.5 to 0.5
Outputs:
- gain_grad: float32 [8, 4096], P('pipe', 'dp')
- first_grad: float32 [8, 4096, 128], P('pipe', 'dp')
- second_grad: float32 [8, 128, 4096], P('pipe', None, 'dp')
The draws below stay inside these ranges and needn't reach their ends.
Inputs may be any that keep to these rules, and one draw needn't show every extreme that they name: `starts`: each row begins with 0 and rises strictly; a micro-batch's documents begin at the first counts entries of its row, the later entries are not used.
All inputs are finite; a program needn't handle non-finite values.
Results may differ from the reference program's by a relative error of at most 0.03.
Values may be sent and summed in bfloat16 or wider, within the bound.
A program may use at most 64 MiB of HBM per device.

```python
import jax
import jax.numpy as jnp
from jax import lax

D = 4096
HD = 128
RANK = 128
SEQ = 32
MB = 2
NDOC = 4
ROWS = 64
LAYERS = 8
N_DP = 32


def draw_starts(key, part):
    start_key = jax.random.fold_in(key, 7001)
    row_keys = jax.random.split(start_key, 2 * ROWS)

    def one_row(row_key):
        picked = jax.random.permutation(row_key, SEQ - 1)[:NDOC - 1].astype(jnp.int32) + 1
        return jnp.concatenate((jnp.zeros((1,), jnp.int32), jnp.sort(picked).astype(jnp.int32)))
    start_table = jax.vmap(one_row)(row_keys).reshape(2, ROWS, NDOC)
    return start_table.at[0, 0, NDOC - 1].set(SEQ - 1)


def draw_counts(key, part):
    count_key = jax.random.fold_in(key, 7002)
    count_table = jax.random.randint(count_key, (2, ROWS), 1, NDOC + 1).astype(jnp.int32)
    return count_table.at[0, 0].set(NDOC).at[1, 0].set(1)


def with_spikes(drawn, own_key, source, target, parts, factor):
    owner, partner = [(jnp.arange(drawn.shape[dim]) // (drawn.shape[dim] // parts)).reshape([-1 if axis == dim else 1 for axis in range(drawn.ndim)]) for dim in (source, target)]
    chosen = jax.random.permutation(own_key, parts)[partner]
    strong = (owner == chosen) | (owner == (partner + parts // 2) % parts)
    return jnp.where(strong, factor * drawn, drawn)


def block_levels(key, extent, cuts, low, high):
    def one(dim, blocks):
        steps = jax.random.uniform(jax.random.fold_in(jax.random.fold_in(key, 6), dim), (blocks,), jnp.float32, low / len(cuts), high / len(cuts))
        return jnp.repeat(jnp.exp(steps), extent[dim] // blocks).reshape((-1,) + (1,) * (len(extent) - dim - 1))

    level = one(*cuts[0])
    for cut in cuts[1:]:
        level = level * one(*cut)
    return level


def normal_values(own_key, shape, deviation, reach, cuts=(), kind=jnp.bfloat16):
    values = deviation * jax.random.normal(own_key, shape, jnp.float32)
    if cuts:
        values = values * block_levels(own_key, shape, cuts, -0.22, 0.18)
    return jnp.clip(values, -reach, reach).astype(kind)


def heavy_noise(stream_key, shape, scale, most, cuts, heavy, kind=jnp.bfloat16):
    drawn = scale * jax.random.normal(stream_key, shape, jnp.float32)
    if cuts:
        drawn = drawn * block_levels(stream_key, shape, cuts, -0.22, 0.18)
    return jnp.clip(with_spikes(drawn, jax.random.fold_in(stream_key, 3), *heavy), -most, most).astype(kind)


def setup_inputs(seed: int = 0) -> dict:
    streams_of = jax.random.split(jax.random.key(seed), 8)
    tokens = normal_values(streams_of[0], (2, ROWS, SEQ, D), 1.0, 6.0, ((1, 32),))
    cotangents = heavy_noise(streams_of[1], (2, ROWS, SEQ, D), 0.05, 1.5, ((1, 32),), (1, 3, 32, 2.75))
    starts = draw_starts(jax.random.fold_in(streams_of[7], 71), 0)
    counts = draw_counts(jax.random.fold_in(streams_of[7], 71), 0)
    layer_gains = jnp.clip(1.0 + 0.1 * jax.random.normal(streams_of[4], (LAYERS, D), jnp.float32), 0.5, 1.5).astype(jnp.bfloat16)
    first_map = normal_values(streams_of[5], (LAYERS, D, RANK), D ** -0.5, 0.09375, ((0, 8), (1, 32)))
    second_map = normal_values(streams_of[6], (LAYERS, RANK, D), RANK ** -0.5, 0.5, ((0, 8), (2, 32)))
    return dict(tokens=tokens, cotangents=cotangents, starts=starts, counts=counts, layer_gains=layer_gains, first_map=first_map, second_map=second_map)


def doc_allowed(row_starts, row_count, length):
    positions = jnp.arange(length, dtype=jnp.int32)
    entries = jnp.arange(row_starts.shape[0], dtype=jnp.int32)
    started = (row_starts[None, :] <= positions[:, None]) & (entries < row_count)[None, :]
    document = lax.optimization_barrier(jnp.sum(started.astype(jnp.int32), axis=1))
    matched = document[:, None] == document[None, :]
    return matched & (positions[None, :] <= positions[:, None])

def apply_layer(activation, gain_row, first_weight, second_weight, allowed):
    length = activation.shape[0]
    model_width = activation.shape[1]
    widened = activation.astype(jnp.float32)
    factor = lax.rsqrt(lax.optimization_barrier(jnp.mean(widened * widened, axis=1, keepdims=True)) + 1e-05)
    normed = (widened * factor * gain_row).astype(jnp.bfloat16)
    split_heads = normed.reshape(length, model_width // HD, HD)
    scores = jnp.einsum('qhd,khd->hqk', split_heads, split_heads, preferred_element_type=jnp.float32) / HD
    weights = jnp.where(allowed[None, :, :], jnp.exp(scores), 0.0)
    probabilities = (weights / lax.optimization_barrier(jnp.sum(weights, axis=2, keepdims=True))).astype(jnp.bfloat16)
    mixed_heads = jnp.einsum('hqk,khd->qhd', probabilities, split_heads, preferred_element_type=jnp.float32)
    mixed_heads = mixed_heads.reshape(length, model_width).astype(jnp.bfloat16)
    reduced = jnp.dot(mixed_heads, first_weight, preferred_element_type=jnp.float32).astype(jnp.bfloat16)
    return (widened + jnp.dot(reduced, second_weight, preferred_element_type=jnp.float32)).astype(jnp.bfloat16)

def layer_chain(gain_all, first_all, second_all, start_tokens, allowed):
    hidden_state = start_tokens
    for layer_index in range(LAYERS):
        hidden_state = apply_layer(hidden_state, gain_all[layer_index], first_all[layer_index], second_all[layer_index], allowed)
    return hidden_state

def reference(tokens, cotangents, starts, counts, layer_gains, first_map, second_map):
    group_total = 2 * N_DP
    token_groups = tokens.reshape(group_total, MB, SEQ, D)
    cot_groups = cotangents.reshape(group_total, MB, SEQ, D)
    start_groups = starts.reshape(group_total, MB, NDOC)
    count_groups = counts.reshape(group_total, MB)
    zero_sums = (jnp.zeros((LAYERS, D), jnp.float32), jnp.zeros((LAYERS, D, RANK), jnp.float32), jnp.zeros((LAYERS, RANK, D), jnp.float32))

    def add_group(running_totals, group_item):
        group_tokens, group_cots, group_starts, group_counts = group_item
        running_sums = zero_sums
        for micro_index in range(MB):
            allowed = doc_allowed(group_starts[micro_index], group_counts[micro_index], SEQ)
            start_tokens = group_tokens[micro_index]
            _, pullback = jax.vjp(lambda gain_in, first_in, second_in: layer_chain(gain_in, first_in, second_in, start_tokens, allowed), layer_gains, first_map, second_map)
            gradients = pullback(group_cots[micro_index])
            running_sums = tuple((current + gradient.astype(jnp.float32) for current, gradient in zip(running_sums, gradients)))
        rounded = tuple((lax.optimization_barrier(current.astype(jnp.bfloat16)).astype(jnp.float32) for current in running_sums))
        return (tuple((current + addition for current, addition in zip(running_totals, rounded))), None)
    totals, _ = lax.scan(add_group, zero_sums, (token_groups, cot_groups, start_groups, count_groups))
    return (totals[0], totals[1], totals[2])
```

```python
import jax
import jax.numpy as jnp
from jax import lax
from jax.experimental import pallas as pl
from jax.experimental.pallas import tpu as pltpu
from jax.sharding import PartitionSpec as P

MESH = pl.DeviceIdType.MESH
F32 = jnp.float32
BF16 = jnp.bfloat16
L = 8
NX = 4
NZ = 8
NY = 4
HD = 128
T = 64
C = 1024
PR = 144
D = 4096


def dot(a, b):
    return lax.dot_general(a, b, (((1,), (0,)), ((), ())), preferred_element_type=F32)


def dot_nt(a, b):
    return lax.dot_general(a, b, (((1,), (1,)), ((), ())), preferred_element_type=F32)


def pair_blocks(v):
    zero = jnp.zeros((T, HD), v.dtype)
    top = jnp.concatenate((v[:, :HD], zero), axis=1)
    low = jnp.concatenate((zero, v[:, HD:]), axis=1)
    return jnp.concatenate((top, low), axis=0)


def token_rows(p):
    both = jnp.concatenate((p, p), axis=0)
    high = both.astype(BF16)
    low = (both - high.astype(F32)).astype(BF16)
    return dot_nt(jnp.ones((16, 2 * HD), BF16), jnp.concatenate((high, low), axis=1))[:8]


def to_column(row):
    return jnp.transpose(jnp.broadcast_to(row[0:1], (HD, HD)))[:T]


def twice(v):
    return jnp.concatenate((v, v), axis=1)


def kernel(
    tok, cot, starts, counts, gain_in, first_in, second_in,
    gain_out, first_out, second_out,
    chunk, wbuf, X, H, M, ES, Fr, R, RR, SS, BB, AA, PS, PT, DYP, MK, MKT,
    G, RA, SA, RB, SB, RC,
    in_sem, s1_send, s1_recv, z_send, z_recv, k_send, k_recv, tp_send, tp_recv,
    a_send, a_recv, b_send, b_recv, c_send, c_recv,
):
    p = lax.axis_index("pipe")
    d = lax.axis_index("dp")
    x, yh = p // 2, p % 2
    yl, z, c = d // 16, (d // 2) % 8, d % 2
    y = 2 * yh + yl
    k_own = z % 4

    def x_peer(i):
        return (((x + i) % NX) * 2 + yh, d)

    def z_peer(zz):
        return (p, yl * 16 + zz * 2 + c)

    core_peer = (p, d + 1 - 2 * c)

    def holder(q):
        yy, h = q // 2, q % 2
        return ((d // 8) * 2 + yy // 2, (yy % 2) * 16 + (2 * k_own + h) * 2 + c)

    def owner(l):
        return (l, 8 * x + 2 * (z // 2) + c)

    def is_me(dev):
        return (dev[0] == p) & (dev[1] == d)

    def remote(src, dst, ss, rs, dev):
        return pltpu.make_async_remote_copy(
            src_ref=src, dst_ref=dst, send_sem=ss, recv_sem=rs, device_id=dev, device_id_type=MESH
        )

    cols = pl.ds(pl.multiple_of(x * C, C), C)
    loads = []
    for b in range(2):
        rows = pl.ds(32 * b, 32)
        loads.append(pltpu.make_async_copy(tok.at[yh, b, :, cols], X.at[0, rows, :], in_sem.at[b]))
        loads.append(pltpu.make_async_copy(cot.at[yh, b, :, cols], M.at[L, rows, :], in_sem.at[2 + b]))
    for load in loads:
        load.start()

    barrier = pltpu.get_barrier_semaphore()

    def greet(dev):
        pl.semaphore_signal(barrier, inc=1, device_id=dev, device_id_type=MESH)

    greet(core_peer)

    def greet_x(i, carry):
        greet(x_peer(i))
        return carry

    def greet_z(i, carry):
        greet(z_peer((z + i) % NZ))
        return carry

    def greet_far(q, carry):
        for dev in (holder(q), owner(q)):
            @pl.when(jnp.logical_not(is_me(dev)))
            def _():
                greet(dev)
        return carry

    lax.fori_loop(1, NX, greet_x, 0)
    lax.fori_loop(1, NZ, greet_z, 0)
    lax.fori_loop(0, 8, greet_far, 0)

    for h in range(2):
        chunk[h, 0:64, :] = first_in[0, 64 * h : 64 * h + 64, :]
        chunk[h, 64:128, :] = second_in[0, 64 * h : 64 * h + 64, :]
        chunk[h, 128:144, :] = jnp.broadcast_to(gain_in[0:1, :].astype(F32), (16, HD)).astype(BF16)

    row_id = lax.broadcasted_iota(jnp.int32, (T, HD), 0)
    lane_id = lax.broadcasted_iota(jnp.int32, (T, HD), 1) % T

    def documents(index):
        second_mb = index >= 32
        pos = jnp.where(second_mb, index - 32, index)
        doc = jnp.zeros((T, HD), jnp.int32)
        count = jnp.where(second_mb, counts[yh, 1], counts[yh, 0])
        for j in range(4):
            start = jnp.where(second_mb, starts[yh, 1, j], starts[yh, 0, j])
            doc = doc + jnp.where((start <= pos) & (j < count), 1, 0)
        return doc + jnp.where(second_mb, 64, 0)

    same = documents(row_id) == documents(lane_id)
    MK[...] = jnp.where(same & (lane_id <= row_id), 1.0, 0.0)
    MKT[...] = jnp.where(same & (row_id <= lane_id), 1.0, 0.0)
    Fr[L] = jnp.zeros((8, HD), F32)
    for i in range(NX):
        BB[L, i] = jnp.zeros((T, HD), BF16)
    half_r = lax.broadcasted_iota(jnp.int32, (HD, HD), 0) // T
    half_l = lax.broadcasted_iota(jnp.int32, (HD, HD), 1) // T
    ones_blocks = jnp.where(half_r == half_l, 1.0, 0.0).astype(BF16)

    me_holder = jnp.int32(0)
    me_owner = jnp.int32(0)
    for q in range(8):
        me_holder = me_holder + jnp.where(is_me(holder(q)), 1, 0)
        me_owner = me_owner + jnp.where(is_me(owner(q)), 1, 0)
    pl.semaphore_wait(barrier, 27 - me_holder - me_owner)

    def s1_copy(q):
        h = q % 2
        return remote(
            chunk.at[h], wbuf.at[p, c, 2 * k_own + h], s1_send.at[q], s1_recv.at[p], holder(q)
        )

    def s1_start(q, carry):
        mine = is_me(holder(q))
        h = q % 2

        @pl.when(mine)
        def _():
            pltpu.make_async_copy(
                chunk.at[h], wbuf.at[p, c, 2 * k_own + h], s1_recv.at[p]
            ).start()

        @pl.when(jnp.logical_not(mine))
        def _():
            s1_copy(q).start()

        return carry

    lax.fori_loop(0, 8, s1_start, 0)

    def tp_copy(kind, buf, e, i):
        slot = buf.at[e, x]
        return remote(slot, slot, tp_send.at[kind, e, i], tp_recv.at[kind, e, x], x_peer(i))

    def tp_send_all(kind, buf, e):
        for i in (2, 1, 3):
            tp_copy(kind, buf, e, i).start()

    def tp_wait(kind, buf, e):
        for i in (1, 3, 2):
            src = (x + i) % NX
            slot = buf.at[e, src]
            remote(slot, slot, tp_send.at[kind, e, i], tp_recv.at[kind, e, src], x_peer(i)).wait_recv()

    def tp_sum(buf, e):
        total = buf[e, 0].astype(F32)
        for i in range(1, NX):
            total = total + buf[e, i].astype(F32)
        return total

    def send_squares(e, value):
        acc = jnp.zeros((T, HD), F32)
        for j in range(C // HD):
            piece = value[:, HD * j : HD * j + HD]
            acc = acc + piece * piece
        SS[e, x] = token_rows(acc)
        tp_send_all(1, SS, e)

    loads[0].wait()
    loads[2].wait()
    send_squares(0, X[0].astype(F32))

    def z_copy(l, i):
        slot = wbuf.at[l, c, z]
        return remote(slot, slot, z_send.at[l, i], z_recv.at[l, z], z_peer((z + i) % NZ))

    def spread(l, carry):
        slot = wbuf.at[l, c, z]
        remote(slot, slot, s1_send.at[0], s1_recv.at[l], core_peer).wait_recv()

        def go(i, inner):
            z_copy(l, i).start()
            return inner

        return lax.fori_loop(1, NZ, go, carry)

    lax.fori_loop(0, L, spread, 0)

    def k_copy(l, which):
        slot = wbuf.at[l, which]
        return remote(slot, slot, k_send.at[l], k_recv.at[l], core_peer)

    def to_core(l):
        def one(i, inner):
            src = (z + i) % NZ
            slot = wbuf.at[l, c, src]
            remote(slot, slot, z_send.at[l, i], z_recv.at[l, src], z_peer(src)).wait_recv()
            return inner

        lax.fori_loop(1, NZ, one, 0)
        k_copy(l, c).start()

    to_core(0)
    to_core(1)

    def w1(l, t):
        return jnp.concatenate(
            [wbuf[l, cc, 2 * t + h, 0:64, :] for cc in range(2) for h in range(2)], axis=0
        )

    def w2(l, t):
        heads = [
            jnp.concatenate([wbuf[l, cc, 2 * t + h, 64:128, :] for h in range(2)], axis=0)
            for cc in range(2)
        ]
        return jnp.concatenate(heads, axis=1)

    def gains(l, t):
        heads = []
        for cc in range(2):
            g16 = wbuf[l, cc, 2 * t, 128:144, :].astype(F32)
            heads.append(jnp.concatenate([g16] * 4, axis=0))
        return jnp.concatenate(heads, axis=1)

    def cols_of(t):
        return slice(256 * t, 256 * t + 256)

    def lanes_of(t):
        return slice(HD * t, HD * t + HD)

    def forward(l, carry):
        k_copy(l, 1 - c).wait_recv()
        raw = []
        for t in range(4):
            h = (X[l, :, cols_of(t)].astype(F32) * gains(l, t)).astype(BF16)
            H[l, :, cols_of(t)] = h
            raw.append(dot_nt(h, pair_blocks(h)))
        tp_wait(1, SS, l)
        f_row = lax.rsqrt(tp_sum(SS, l) * (1.0 / D) + 1e-05)
        Fr[l] = f_row
        f_key = f_row[0:1]
        scale = to_column(f_row) * f_key * (1.0 / HD)
        mask = MK[...]
        part = jnp.zeros((T, HD), F32)
        for t in range(4):
            e = jnp.exp(raw[t] * scale).astype(BF16)
            ES[l, :, lanes_of(t)] = e
            e = (e.astype(F32) * mask).astype(BF16)
            sums = dot(e, ones_blocks)
            prob = (e.astype(F32) * f_key / sums).astype(BF16)
            mixed = dot(prob, pair_blocks(H[l, :, cols_of(t)])).astype(BF16)
            M[l, :, cols_of(t)] = mixed
            part = part + dot(mixed, w1(l, t))
        RR[l, x] = part.astype(BF16)
        tp_send_all(0, RR, l)

        @pl.when(l > 0)
        def _():
            cross = jnp.zeros((T, HD), F32)
            for t in range(4):
                cross = cross + dot_nt(X[l, :, cols_of(t)], w2(l - 1, t))
            BB[l, x] = cross.astype(BF16)
            tp_send_all(2, BB, l)

        @pl.when(l == L - 1)
        def _():
            loads[1].wait()
            loads[3].wait()
            acc = jnp.zeros((T, HD), F32)
            for t in range(4):
                acc = acc + dot_nt(M[L, :, cols_of(t)], w2(L - 1, t))
            AA[L - 1, x, 0:64, :] = acc.astype(BF16)
            AA[L - 1, x, 64:80, :] = jnp.zeros((16, HD), BF16)
            tp_send_all(3, AA, L - 1)
            DYP[...] = M[L].astype(F32)

        @pl.when(l + 2 < L)
        def _():
            to_core(l + 2)

        tp_wait(0, RR, l)
        r = tp_sum(RR, l).astype(BF16)
        R[l] = r
        for t in range(4):
            X[l + 1, :, cols_of(t)] = (
                X[l, :, cols_of(t)].astype(F32) + dot(r, w2(l, t))
            ).astype(BF16)

        @pl.when(l < L - 1)
        def _():
            send_squares(l + 1, X[l + 1].astype(F32))

        return carry

    lax.fori_loop(0, L, forward, 0)

    def a_copy(l, which):
        return remote(G.at[l, which], RA.at[l], a_send.at[l], a_recv.at[l], core_peer)

    def b_copy(l, i):
        zz = (z + i) % NZ
        return remote(SA.at[l, zz], RB.at[l, z], b_send.at[l, i], b_recv.at[l, z], z_peer(zz))

    def c_copy(l):
        return remote(SB.at[l], RC.at[y, z % 2], c_send.at[l], c_recv.at[y, z % 2], owner(l))

    def one_layer(l):
        f_row = Fr[l]
        f_key = f_row[0:1]
        f_col = to_column(f_row)
        mask = MK[...]
        mask_t = MKT[...]
        for t in range(4):
            es = ES[l, :, lanes_of(t)].astype(F32)
            e = es * mask
            sums = dot(e.astype(BF16), ones_blocks)
            PS[:, lanes_of(t)] = e / sums
            et = es * mask_t
            PT[:, lanes_of(t)] = et / jnp.sum(et, axis=0, keepdims=True)

        @pl.when(l < L - 1)
        def _():
            tp_wait(2, BB, l + 1)

        tp_wait(3, AA, l)
        total = tp_sum(AA, l)
        s_row = total[64:72] + total[72:80]
        f_next = Fr[l + 1]
        coef = to_column(f_next * f_next * f_next * s_row * (1.0 / D))
        dr = total[:64] - coef * tp_sum(BB, l + 1)
        dr_b = dr.astype(BF16)
        coef2 = twice(coef)
        f_col2 = twice(f_col)
        s_part = jnp.zeros((T, HD), F32)
        acc = jnp.zeros((T, HD), F32)
        below = jnp.maximum(l - 1, 0)
        for t in range(4):
            h = H[l, :, cols_of(t)]
            blocks = pair_blocks(h)
            dm = dot_nt(dr_b, w1(l, t)).astype(BF16)
            dm_blocks = pair_blocks(dm)
            prob = PS[:, lanes_of(t)]
            prob_t = PT[:, lanes_of(t)]
            dp = dot_nt(dm, blocks) * f_key
            dp_t = dot_nt(h, dm_blocks) * f_col
            inner = dot((prob * dp).astype(BF16), ones_blocks)
            ds = prob * (dp - inner)
            inner_t = jnp.sum(prob_t * dp_t, axis=0, keepdims=True)
            ds_t = prob_t * (dp_t - inner_t)
            both = (ds + ds_t) * f_key * (1.0 / HD)
            left = jnp.concatenate((both.astype(BF16), prob_t.astype(BF16)), axis=1)
            dn = dot(left, jnp.concatenate((blocks, dm_blocks), axis=0))
            xs = X[l, :, cols_of(t)].astype(F32)
            gdn = dn * gains(l, t)
            dy = DYP[:, cols_of(t)] - X[l + 1, :, cols_of(t)].astype(F32) * coef2
            M[L, :, cols_of(t)] = dy.astype(BF16)
            dyp = dy + gdn * f_col2
            DYP[:, cols_of(t)] = dyp
            acc = acc + dot_nt(dyp.astype(BF16), w2(below, t))
            prod = gdn * xs
            s_part = s_part + prod[:, :HD] + prod[:, HD:]
            dgain = jnp.sum(dn * xs * f_col2, axis=0, keepdims=True)
            wide = jnp.broadcast_to(dgain, (16, 256)).astype(BF16)
            for cc in range(2):
                for h2 in range(2):
                    G[l, cc, 2 * t + h2, 128:144, :] = wide[:, HD * cc : HD * cc + HD]

        @pl.when(l > 0)
        def _():
            s_new = token_rows(s_part)
            s_high = s_new.astype(BF16).astype(F32)
            AA[below, x, 0:64, :] = acc.astype(BF16)
            AA[below, x, 64:80, :] = jnp.concatenate((s_high, s_new - s_high), axis=0).astype(BF16)
            tp_send_all(3, AA, below)

        zeros = jnp.zeros((T, HD), F32)
        dr_t = jnp.transpose(jnp.concatenate((dr, zeros), axis=0)).astype(BF16)[:, :T]
        r_t = jnp.transpose(jnp.concatenate((R[l].astype(F32), zeros), axis=0)).astype(BF16)[:, :T]
        for t in range(4):
            g1 = dot(dr_t, M[l, :, cols_of(t)]).astype(BF16)
            g2 = dot(r_t, M[L, :, cols_of(t)]).astype(BF16)
            for cc in range(2):
                for h2 in range(2):
                    rows = slice(64 * h2, 64 * h2 + 64)
                    lanes = slice(HD * cc, HD * cc + HD)
                    G[l, cc, 2 * t + h2, 0:64, :] = g1[rows, lanes]
                    G[l, cc, 2 * t + h2, 64:128, :] = g2[rows, lanes]
        a_copy(l, 1 - c).start()

    def core_sums(l):
        a_copy(l, 1 - c).wait_recv()

        def one(i, carry):
            SA[l, i] = (G[l, c, i].astype(F32) + RA[l, i].astype(F32)).astype(BF16)
            return carry

        lax.fori_loop(0, NZ, one, 0)
        RB[l, z] = SA[l, z]

        def go(i, carry):
            b_copy(l, i).start()
            return carry

        lax.fori_loop(1, NZ, go, 0)

    def z_sums(l):
        def one(i, carry):
            src = (z + i) % NZ
            remote(
                SA.at[l, src], RB.at[l, src], b_send.at[l, i], b_recv.at[l, src], z_peer(src)
            ).wait_recv()
            return carry

        lax.fori_loop(1, NZ, one, 0)
        total = RB[l, 0].astype(F32)
        for i in range(1, NZ):
            total = total + RB[l, i].astype(F32)
        SB[l] = total.astype(BF16)
        mine = is_me(owner(l))

        @pl.when(mine)
        def _():
            pltpu.make_async_copy(SB.at[l], RC.at[y, z % 2], c_recv.at[y, z % 2]).start()

        @pl.when(jnp.logical_not(mine))
        def _():
            c_copy(l).start()

    def backward(i, carry):
        @pl.when(i < L)
        def _():
            one_layer(L - 1 - i)

        @pl.when((i >= 1) & (i < L + 1))
        def _():
            core_sums(L - i)

        @pl.when(i >= 2)
        def _():
            z_sums(L + 1 - i)

        return carry

    lax.fori_loop(0, L + 2, backward, 0)

    for yy in range(NY):
        for h in range(2):
            remote(
                SB.at[0], RC.at[yy, h], c_send.at[0], c_recv.at[yy, h], core_peer
            ).wait_recv()
    halves = []
    for h in range(2):
        total = RC[0, h].astype(F32)
        for yy in range(1, NY):
            total = total + RC[yy, h].astype(F32)
        halves.append(total)
    first_out[0] = jnp.transpose(jnp.concatenate((halves[0][0:64], halves[1][0:64]), axis=0))
    second_out[0] = jnp.concatenate((halves[0][64:128], halves[1][64:128]), axis=0)
    gain_out[...] = halves[0][128:129]

    def drain_far(q, carry):
        @pl.when(jnp.logical_not(is_me(holder(q))))
        def _():
            s1_copy(q).wait_send()

        @pl.when(jnp.logical_not(is_me(owner(q))))
        def _():
            c_copy(q).wait_send()

        return carry

    lax.fori_loop(0, 8, drain_far, 0)

    def drain(l, carry):
        k_copy(l, c).wait_send()
        a_copy(l, 1 - c).wait_send()
        for i in range(1, NX):
            tp_copy(0, RR, l, i).wait_send()
            tp_copy(1, SS, l, i).wait_send()
            tp_copy(3, AA, l, i).wait_send()

            @pl.when(l > 0)
            def _():
                tp_copy(2, BB, l, i).wait_send()

        def one(i, inner):
            z_copy(l, i).wait_send()
            b_copy(l, i).wait_send()
            return inner

        return lax.fori_loop(1, NZ, one, carry)

    lax.fori_loop(0, L, drain, 0)


def per_device(tokens, cotangents, starts, counts, layer_gains, first_map, second_map):
    vmem = pl.BlockSpec(memory_space=pltpu.VMEM)
    smem = pl.BlockSpec(memory_space=pltpu.SMEM)
    hbm = pl.BlockSpec(memory_space=pl.ANY)
    sem = pltpu.SemaphoreType.DMA
    return pl.pallas_call(
        kernel,
        out_shape=(
            jax.ShapeDtypeStruct((1, HD), F32),
            jax.ShapeDtypeStruct((1, HD, HD), F32),
            jax.ShapeDtypeStruct((1, HD, HD), F32),
        ),
        in_specs=[hbm, hbm, smem, smem, vmem, vmem, vmem],
        out_specs=(vmem, vmem, vmem),
        scratch_shapes=[
            pltpu.VMEM((2, PR, HD), BF16),
            pltpu.VMEM((L, 2, NZ, PR, HD), BF16),
            pltpu.VMEM((L + 1, T, C), BF16),
            pltpu.VMEM((L, T, C), BF16),
            pltpu.VMEM((L + 1, T, C), BF16),
            pltpu.VMEM((L, T, 4 * HD), BF16),
            pltpu.VMEM((L + 1, 8, HD), F32),
            pltpu.VMEM((L, T, HD), BF16),
            pltpu.VMEM((L, NX, T, HD), BF16),
            pltpu.VMEM((L, NX, 8, HD), F32),
            pltpu.VMEM((L + 1, NX, T, HD), BF16),
            pltpu.VMEM((L, NX, 80, HD), BF16),
            pltpu.VMEM((T, 4 * HD), F32),
            pltpu.VMEM((T, 4 * HD), F32),
            pltpu.VMEM((T, C), F32),
            pltpu.VMEM((T, HD), F32),
            pltpu.VMEM((T, HD), F32),
            pltpu.VMEM((L, 2, NZ, PR, HD), BF16),
            pltpu.VMEM((L, NZ, PR, HD), BF16),
            pltpu.VMEM((L, NZ, PR, HD), BF16),
            pltpu.VMEM((L, NZ, PR, HD), BF16),
            pltpu.VMEM((L, PR, HD), BF16),
            pltpu.VMEM((NY, 2, PR, HD), BF16),
            sem((4,)),
            sem((8,)), sem((L,)),
            sem((L, NZ)), sem((L, NZ)),
            sem((L,)), sem((L,)),
            sem((4, L, NX)), sem((4, L, NX)),
            sem((L,)), sem((L,)),
            sem((L, NZ)), sem((L, NZ)),
            sem((L,)), sem((NY, 2)),
        ],
        compiler_params=pltpu.CompilerParams(
            collective_id=0, has_side_effects=True, vmem_limit_bytes=48 * 1024 * 1024
        ),
    )(tokens, cotangents, starts, counts, layer_gains, first_map, second_map)


def solution(mesh):
    in_specs = (
        P(None, "dp", None, None),
        P(None, "dp", None, None),
        P(None, "dp", None),
        P(None, "dp"),
        P("pipe", "dp"),
        P("pipe", "dp", None),
        P("pipe", None, "dp"),
    )
    out_specs = (P("pipe", "dp"), P("pipe", "dp", None), P("pipe", None, "dp"))
    return jax.shard_map(
        per_device, mesh=mesh, in_specs=in_specs, out_specs=out_specs, check_vma=False
    )
```

```python
import jax
import jax.numpy as jnp
from jax import lax
from jax.experimental import pallas as pl
from jax.experimental.pallas import tpu as pltpu
from jax.sharding import PartitionSpec as P

MESH = pl.DeviceIdType.MESH
F32 = jnp.float32
BF16 = jnp.bfloat16
L = 8
NX = 4
NZ = 8
NY = 4
HD = 128
T = 64
C = 1024
PR = 40
D = 4096
VMEM_LIMIT = 67043328 - 136 * 1024


def dot(a, b):
    return lax.dot_general(a, b, (((1,), (0,)), ((), ())), preferred_element_type=F32)


def dot_nt(a, b):
    return lax.dot_general(a, b, (((1,), (1,)), ((), ())), preferred_element_type=F32)


def pair_blocks(v):
    zero = jnp.zeros((T, HD), v.dtype)
    top = jnp.concatenate((v[:, :HD], zero), axis=1)
    low = jnp.concatenate((zero, v[:, HD:]), axis=1)
    return jnp.concatenate((top, low), axis=0)


def token_rows(p):
    both = jnp.concatenate((p, p), axis=0)
    high = both.astype(BF16)
    low = (both - high.astype(F32)).astype(BF16)
    return dot_nt(jnp.ones((16, 2 * HD), BF16), jnp.concatenate((high, low), axis=1))[:8]


def to_column(row):
    return jnp.transpose(jnp.broadcast_to(row[0:1], (HD, HD)))[:T]


def twice(v):
    return jnp.concatenate((v, v), axis=1)


def kernel(
    tok, cot, starts, counts, gain_in, first_in, second_in,
    gain_out, first_out, second_out,
    chunk, own_gain, own_first, own_second, wbuf, X, H, M, ES, Fr, R, RR, SS, BB, AA,
    PS, PT, DYP, MK, MKT, G, RA, SA, RB, SB, RC, SD, RD,
    in_sem, sent, s1_recv, z_recv, y_recv, k_recv, tp_recv, b_recv,
    ga_recv, gy_recv, gz_recv, go_recv,
):
    p = lax.axis_index("pipe")
    d = lax.axis_index("dp")
    x, yh = p // 2, p % 2
    yl, z, c = d // 16, (d // 2) % 8, d % 2
    y = 2 * yh + yl
    k_own = z % 4

    def x_peer(i):
        return (((x + i) % NX) * 2 + yh, d)

    def z_peer(zz):
        return (p, yl * 16 + zz * 2 + c)

    def y_peer(yy):
        return (x * 2 + yy // 2, (yy % 2) * 16 + z * 2 + c)

    core_peer = (p, d + 1 - 2 * c)

    def holder(q):
        yy, h = q // 2, q % 2
        return ((d // 8) * 2 + yy // 2, (yy % 2) * 16 + (2 * k_own + h) * 2 + c)

    def owner(l):
        return (l, 8 * x + 2 * (z // 2) + c)

    def is_me(dev):
        return (dev[0] == p) & (dev[1] == d)

    def arrived(ref, sem):
        pltpu.make_async_copy(ref, ref, sem).wait()

    def remote(src, dst, ss, rs, dev):
        return pltpu.make_async_remote_copy(
            src_ref=src, dst_ref=dst, send_sem=ss, recv_sem=rs, device_id=dev, device_id_type=MESH
        )

    cols = pl.ds(pl.multiple_of(x * C, C), C)
    loads = []
    for b in range(2):
        rows = pl.ds(32 * b, 32)
        loads.append(pltpu.make_async_copy(tok.at[yh, b, :, cols], X.at[0, rows, :], in_sem.at[b]))
        loads.append(pltpu.make_async_copy(cot.at[yh, b, :, cols], M.at[L, rows, :], in_sem.at[2 + b]))
    chunk_loads = [
        pltpu.make_async_copy(first_in, own_first, in_sem.at[4]),
        pltpu.make_async_copy(second_in, own_second, in_sem.at[5]),
        pltpu.make_async_copy(gain_in, own_gain, in_sem.at[6]),
    ]
    for load in chunk_loads + loads:
        load.start()

    barrier = pltpu.get_barrier_semaphore()

    def greet(dev):
        pl.semaphore_signal(barrier, inc=1, device_id=dev, device_id_type=MESH)

    def greet_x(i, carry):
        greet(x_peer(i))
        return carry

    def greet_z(i, carry):
        greet(z_peer((z + i) % NZ))
        return carry

    def greet_y(i, carry):
        greet(y_peer((y + i) % NY))
        return carry

    def greet_far(q, carry):
        for dev in (holder(q), owner(q)):
            @pl.when(jnp.logical_not(is_me(dev)))
            def _():
                greet(dev)
        return carry

    lax.fori_loop(0, 8, greet_far, 0)
    lax.fori_loop(1, NZ, greet_z, 0)
    lax.fori_loop(1, NY, greet_y, 0)
    lax.fori_loop(1, NX, greet_x, 0)
    greet(core_peer)

    row_id = lax.broadcasted_iota(jnp.int32, (T, HD), 0)
    lane_id = lax.broadcasted_iota(jnp.int32, (T, HD), 1) % T

    def documents(index):
        second_mb = index >= 32
        pos = jnp.where(second_mb, index - 32, index)
        doc = jnp.zeros((T, HD), jnp.int32)
        count = jnp.where(second_mb, counts[yh, 1], counts[yh, 0])
        for j in range(4):
            start = jnp.where(second_mb, starts[yh, 1, j], starts[yh, 0, j])
            doc = doc + jnp.where((start <= pos) & (j < count), 1, 0)
        return doc + jnp.where(second_mb, 64, 0)

    same = documents(row_id) == documents(lane_id)
    MK[...] = jnp.where(same & (lane_id <= row_id), 1.0, 0.0)
    MKT[...] = jnp.where(same & (row_id <= lane_id), 1.0, 0.0)
    Fr[L] = jnp.zeros((8, HD), F32)
    for i in range(NX):
        BB[L, i] = jnp.zeros((T, HD), BF16)
    half_r = lax.broadcasted_iota(jnp.int32, (HD, HD), 0) // T
    half_l = lax.broadcasted_iota(jnp.int32, (HD, HD), 1) // T
    ones_blocks = jnp.where(half_r == half_l, 1.0, 0.0).astype(BF16)

    me_holder = jnp.int32(0)
    me_owner = jnp.int32(0)
    for q in range(8):
        me_holder = me_holder + jnp.where(is_me(holder(q)), 1, 0)
        me_owner = me_owner + jnp.where(is_me(owner(q)), 1, 0)
    for load in chunk_loads:
        load.wait()
    for q in range(8):
        rows = slice(64 * (q % 2) + 16 * (q // 2), 64 * (q % 2) + 16 * (q // 2) + 16)
        chunk[q, 0:16, :] = own_first[0, rows, :]
        chunk[q, 16:32, :] = own_second[0, rows, :]
        chunk[q, 32:40, :] = jnp.broadcast_to(own_gain[0:1, :].astype(F32), (8, HD)).astype(BF16)
    pl.semaphore_wait(barrier, 30 - me_holder - me_owner)

    def s1_start(q, carry):
        mine = is_me(holder(q))
        slot = wbuf.at[p, c, q // 2, 2 * k_own + q % 2]

        @pl.when(mine)
        def _():
            pltpu.make_async_copy(chunk.at[q], slot, s1_recv.at[p]).start()

        @pl.when(jnp.logical_not(mine))
        def _():
            remote(chunk.at[q], slot, sent.at[0], s1_recv.at[p], holder(q)).start()

        return carry

    lax.fori_loop(0, 8, s1_start, 0)

    def tp_send_all(kind, buf, e, sem):
        slot = buf.at[e, x]
        for i in (2, 1, 3):
            remote(slot, slot, sent.at[kind], sem, x_peer(i)).start()

    def tp_wait(buf, e, sem):
        arrived(buf.at[e, 0 : NX - 1], sem)

    def tp_sum(buf, e):
        total = buf[e, 0].astype(F32)
        for i in range(1, NX):
            total = total + buf[e, i].astype(F32)
        return total

    def send_squares(e, value):
        acc = jnp.zeros((T, HD), F32)
        for j in range(C // HD):
            piece = value[:, HD * j : HD * j + HD]
            acc = acc + piece * piece
        SS[e, x] = token_rows(acc)
        tp_send_all(2, SS, e, tp_recv.at[1, e % 2])

    loads[0].wait()
    loads[2].wait()
    send_squares(0, X[0].astype(F32))

    def spread(l, carry):
        slot = wbuf.at[l, c, y, z]
        arrived(slot, s1_recv.at[l])

        def go(i, inner):
            remote(slot, slot, sent.at[5], z_recv.at[l], z_peer((z + i) % NZ)).start()
            return inner

        return lax.fori_loop(1, NZ, go, carry)

    lax.fori_loop(0, L, spread, 0)

    def along_y(l):
        arrived(wbuf.at[l, c, y, 0 : NZ - 1], z_recv.at[l])
        slot = wbuf.at[l, c, y]
        for i in (2, 1, 3):
            remote(slot, slot, sent.at[6], y_recv.at[l], y_peer((y + i) % NY)).start()

    def to_core(l):
        arrived(wbuf.at[l, c, 0 : NY - 1], y_recv.at[l])
        slot = wbuf.at[l, c]
        remote(slot, slot, sent.at[7], k_recv.at[l], core_peer).start()

    along_y(0)
    along_y(1)
    to_core(0)

    def w1(l, t):
        return jnp.concatenate(
            [
                wbuf[l, cc, yy, 2 * t + h, 0:16, :]
                for cc in range(2) for h in range(2) for yy in range(NY)
            ],
            axis=0,
        )

    def w2(l, t):
        heads = [
            jnp.concatenate(
                [wbuf[l, cc, yy, 2 * t + h, 16:32, :] for h in range(2) for yy in range(NY)], axis=0
            )
            for cc in range(2)
        ]
        return jnp.concatenate(heads, axis=1)

    def gains(l, t):
        heads = []
        for cc in range(2):
            g8 = wbuf[l, cc, 0, 2 * t, 32:40, :].astype(F32)
            heads.append(jnp.concatenate([g8] * 8, axis=0))
        return jnp.concatenate(heads, axis=1)

    def cols_of(t):
        return slice(256 * t, 256 * t + 256)

    def lanes_of(t):
        return slice(HD * t, HD * t + HD)

    def forward(l, carry):
        arrived(wbuf.at[l, c], k_recv.at[l])
        raw = []
        for t in range(4):
            h = (X[l, :, cols_of(t)].astype(F32) * gains(l, t)).astype(BF16)
            H[l, :, cols_of(t)] = h
            raw.append(dot_nt(h, pair_blocks(h)))
        tp_wait(SS, l, tp_recv.at[1, l % 2])
        f_row = lax.rsqrt(tp_sum(SS, l) * (1.0 / D) + 1e-05)
        Fr[l] = f_row
        f_key = f_row[0:1]
        scale = to_column(f_row) * f_key * (1.0 / HD)
        mask = MK[...]
        part = jnp.zeros((T, HD), F32)
        for t in range(4):
            e = jnp.exp(raw[t] * scale).astype(BF16)
            ES[l, :, lanes_of(t)] = e
            e = (e.astype(F32) * mask).astype(BF16)
            sums = dot(e, ones_blocks)
            prob = (e.astype(F32) * f_key / sums).astype(BF16)
            mixed = dot(prob, pair_blocks(H[l, :, cols_of(t)])).astype(BF16)
            M[l, :, cols_of(t)] = mixed
            part = part + dot(mixed, w1(l, t))
        RR[l, x] = part.astype(BF16)
        tp_send_all(1, RR, l, tp_recv.at[0, l % 2])

        @pl.when(l > 0)
        def _():
            cross = jnp.zeros((T, HD), F32)
            for t in range(4):
                cross = cross + dot_nt(X[l, :, cols_of(t)], w2(l - 1, t))
            BB[l, x] = cross.astype(BF16)
            tp_send_all(3, BB, l, b_recv.at[0])

        @pl.when(l == L - 1)
        def _():
            loads[1].wait()
            loads[3].wait()
            acc = jnp.zeros((T, HD), F32)
            for t in range(4):
                acc = acc + dot_nt(M[L, :, cols_of(t)], w2(L - 1, t))
            AA[L - 1, x, 0:64, :] = acc.astype(BF16)
            AA[L - 1, x, 64:80, :] = jnp.zeros((16, HD), BF16)
            tp_send_all(4, AA, L - 1, tp_recv.at[2, (L - 1) % 2])
            DYP[...] = M[L].astype(F32)

        @pl.when(l + 1 < L)
        def _():
            to_core(l + 1)

        @pl.when(l + 2 < L)
        def _():
            along_y(l + 2)

        tp_wait(RR, l, tp_recv.at[0, l % 2])
        r = tp_sum(RR, l).astype(BF16)
        R[l] = r
        for t in range(4):
            X[l + 1, :, cols_of(t)] = (
                X[l, :, cols_of(t)].astype(F32) + dot(r, w2(l, t))
            ).astype(BF16)

        @pl.when(l < L - 1)
        def _():
            send_squares(l + 1, X[l + 1].astype(F32))

        return carry

    lax.fori_loop(0, L, forward, 0)

    def one_layer(l):
        f_row = Fr[l]
        f_key = f_row[0:1]
        f_col = to_column(f_row)
        mask = MK[...]
        mask_t = MKT[...]
        for t in range(4):
            es = ES[l, :, lanes_of(t)].astype(F32)
            e = es * mask
            sums = dot(e.astype(BF16), ones_blocks)
            PS[:, lanes_of(t)] = e / sums
            et = es * mask_t
            PT[:, lanes_of(t)] = et / jnp.sum(et, axis=0, keepdims=True)

        @pl.when(l == L - 1)
        def _():
            arrived(BB.at[1:L, 0 : NX - 1], b_recv.at[0])

        tp_wait(AA, l, tp_recv.at[2, l % 2])
        total = tp_sum(AA, l)
        s_row = total[64:72] + total[72:80]
        f_next = Fr[l + 1]
        coef = to_column(f_next * f_next * f_next * s_row * (1.0 / D))
        dr = total[:64] - coef * tp_sum(BB, l + 1)
        dr_b = dr.astype(BF16)
        coef2 = twice(coef)
        f_col2 = twice(f_col)
        s_part = jnp.zeros((T, HD), F32)
        acc = jnp.zeros((T, HD), F32)
        below = jnp.maximum(l - 1, 0)
        for t in range(4):
            h = H[l, :, cols_of(t)]
            blocks = pair_blocks(h)
            dm = dot_nt(dr_b, w1(l, t)).astype(BF16)
            dm_blocks = pair_blocks(dm)
            prob = PS[:, lanes_of(t)]
            prob_t = PT[:, lanes_of(t)]
            dp = dot_nt(dm, blocks) * f_key
            dp_t = dot_nt(h, dm_blocks) * f_col
            inner = dot((prob * dp).astype(BF16), ones_blocks)
            ds = prob * (dp - inner)
            inner_t = jnp.sum(prob_t * dp_t, axis=0, keepdims=True)
            ds_t = prob_t * (dp_t - inner_t)
            both = (ds + ds_t) * f_key * (1.0 / HD)
            left = jnp.concatenate((both.astype(BF16), prob_t.astype(BF16)), axis=1)
            dn = dot(left, jnp.concatenate((blocks, dm_blocks), axis=0))
            xs = X[l, :, cols_of(t)].astype(F32)
            gdn = dn * gains(l, t)
            dy = DYP[:, cols_of(t)] - X[l + 1, :, cols_of(t)].astype(F32) * coef2
            M[L, :, cols_of(t)] = dy.astype(BF16)
            dyp = dy + gdn * f_col2
            DYP[:, cols_of(t)] = dyp
            acc = acc + dot_nt(dyp.astype(BF16), w2(below, t))
            prod = gdn * xs
            s_part = s_part + prod[:, :HD] + prod[:, HD:]
            dgain = jnp.sum(dn * xs * f_col2, axis=0, keepdims=True)
            wide = jnp.broadcast_to(dgain, (8, 256)).astype(BF16)
            for cc in range(2):
                for h2 in range(2):
                    for yy in range(NY):
                        G[l, cc, yy, 2 * t + h2, 32:40, :] = wide[:, HD * cc : HD * cc + HD]

        @pl.when(l > 0)
        def _():
            s_new = token_rows(s_part)
            s_high = s_new.astype(BF16).astype(F32)
            AA[below, x, 0:64, :] = acc.astype(BF16)
            AA[below, x, 64:80, :] = jnp.concatenate((s_high, s_new - s_high), axis=0).astype(BF16)
            tp_send_all(4, AA, below, tp_recv.at[2, below % 2])

        zeros = jnp.zeros((T, HD), F32)
        dr_t = jnp.transpose(jnp.concatenate((dr, zeros), axis=0)).astype(BF16)[:, :T]
        r_t = jnp.transpose(jnp.concatenate((R[l].astype(F32), zeros), axis=0)).astype(BF16)[:, :T]
        for t in range(4):
            g1 = dot(dr_t, M[l, :, cols_of(t)]).astype(BF16)
            g2 = dot(r_t, M[L, :, cols_of(t)]).astype(BF16)
            for cc in range(2):
                for q in range(8):
                    rows = slice(64 * (q % 2) + 16 * (q // 2), 64 * (q % 2) + 16 * (q // 2) + 16)
                    lanes = slice(HD * cc, HD * cc + HD)
                    G[l, cc, q // 2, 2 * t + q % 2, 0:16, :] = g1[rows, lanes]
                    G[l, cc, q // 2, 2 * t + q % 2, 16:32, :] = g2[rows, lanes]
        remote(G.at[l, 1 - c], RA.at[l], sent.at[8], ga_recv.at[l], core_peer).start()

    def core_sums(l):
        arrived(RA.at[l], ga_recv.at[l])

        def one(i, carry):
            SA[l, i] = (G[l, c, i].astype(F32) + RA[l, i].astype(F32)).astype(BF16)
            return carry

        lax.fori_loop(0, NY, one, 0)
        RB[l, y] = SA[l, y]
        for i in (2, 1, 3):
            yy = (y + i) % NY
            remote(SA.at[l, yy], RB.at[l, y], sent.at[9], gy_recv.at[l], y_peer(yy)).start()

    def y_sums(l):
        arrived(RB.at[l, 0 : NY - 1], gy_recv.at[l])
        total = RB[l, 0].astype(F32)
        for i in range(1, NY):
            total = total + RB[l, i].astype(F32)
        SB[l] = total.astype(BF16)
        RC[l, z] = SB[l, z]

        def go(i, carry):
            zz = (z + i) % NZ
            remote(SB.at[l, zz], RC.at[l, z], sent.at[10], gz_recv.at[l], z_peer(zz)).start()
            return carry

        lax.fori_loop(1, NZ, go, 0)

    def z_sums(l):
        arrived(RC.at[l, 0 : NZ - 1], gz_recv.at[l])
        total = RC[l, 0].astype(F32)
        for i in range(1, NZ):
            total = total + RC[l, i].astype(F32)
        SD[l] = total.astype(BF16)
        mine = is_me(owner(l))

        @pl.when(mine)
        def _():
            pltpu.make_async_copy(SD.at[l], RD.at[y, z % 2], go_recv.at[0]).start()

        @pl.when(jnp.logical_not(mine))
        def _():
            remote(SD.at[l], RD.at[y, z % 2], sent.at[11], go_recv.at[0], owner(l)).start()

    def backward(i, carry):
        @pl.when(i < L)
        def _():
            one_layer(L - 1 - i)

        @pl.when((i >= 1) & (i < L + 1))
        def _():
            core_sums(L - i)

        @pl.when((i >= 2) & (i < L + 2))
        def _():
            y_sums(L + 1 - i)

        @pl.when(i >= 3)
        def _():
            z_sums(L + 2 - i)

        return carry

    lax.fori_loop(0, L + 3, backward, 0)

    arrived(RD, go_recv.at[0])
    grads = []
    for part in range(2):
        rows = slice(16 * part, 16 * part + 16)
        blocks = [RD[yy, h, rows, :].astype(F32) for h in range(2) for yy in range(NY)]
        grads.append(jnp.concatenate(blocks, axis=0))
    first_out[0] = jnp.transpose(grads[0])
    second_out[0] = grads[1]
    gain_out[...] = RD[0, 0, 32:40, :].astype(F32)[0:1]

    for used, sem, pieces in ((me_holder, 0, chunk), (me_owner, 11, SD)):
        @pl.when(used > 0)
        def _():
            arrived(pieces.at[0:7], sent.at[sem])

        @pl.when(used == 0)
        def _():
            arrived(pieces, sent.at[sem])

    arrived(RR.at[0:6], sent.at[1])
    arrived(SS.at[0:6], sent.at[2])
    arrived(BB.at[0:7, 0:3], sent.at[3])
    arrived(AA.at[0:6], sent.at[4])
    arrived(wbuf.at[0:7, 0, 0], sent.at[5])
    arrived(wbuf.at[0:3], sent.at[6])
    arrived(wbuf.at[0:4], sent.at[7])
    arrived(G.at[0:4], sent.at[8])
    arrived(SA.at[0:6], sent.at[9])
    arrived(SB.at[0:7], sent.at[10])


def per_device(tokens, cotangents, starts, counts, layer_gains, first_map, second_map):
    vmem = pl.BlockSpec(memory_space=pltpu.VMEM)
    smem = pl.BlockSpec(memory_space=pltpu.SMEM)
    hbm = pl.BlockSpec(memory_space=pl.ANY)
    sem = pltpu.SemaphoreType.DMA
    return pl.pallas_call(
        kernel,
        out_shape=(
            jax.ShapeDtypeStruct((1, HD), F32),
            jax.ShapeDtypeStruct((1, HD, HD), F32),
            jax.ShapeDtypeStruct((1, HD, HD), F32),
        ),
        in_specs=[hbm, hbm, smem, smem, hbm, hbm, hbm],
        out_specs=(vmem, vmem, vmem),
        scratch_shapes=[
            pltpu.VMEM((8, PR, HD), BF16),
            pltpu.VMEM((1, HD), BF16),
            pltpu.VMEM((1, HD, HD), BF16),
            pltpu.VMEM((1, HD, HD), BF16),
            pltpu.VMEM((L, 2, NY, NZ, PR, HD), BF16),
            pltpu.VMEM((L + 1, T, C), BF16),
            pltpu.VMEM((L, T, C), BF16),
            pltpu.VMEM((L + 1, T, C), BF16),
            pltpu.VMEM((L, T, 4 * HD), BF16),
            pltpu.VMEM((L + 1, 8, HD), F32),
            pltpu.VMEM((L, T, HD), BF16),
            pltpu.VMEM((L, NX, T, HD), BF16),
            pltpu.VMEM((L, NX, 8, HD), F32),
            pltpu.VMEM((L + 1, NX, T, HD), BF16),
            pltpu.VMEM((L, NX, 80, HD), BF16),
            pltpu.VMEM((T, 4 * HD), F32),
            pltpu.VMEM((T, 4 * HD), F32),
            pltpu.VMEM((T, C), F32),
            pltpu.VMEM((T, HD), F32),
            pltpu.VMEM((T, HD), F32),
            pltpu.VMEM((L, 2, NY, NZ, PR, HD), BF16),
            pltpu.VMEM((L, NY, NZ, PR, HD), BF16),
            pltpu.VMEM((L, NY, NZ, PR, HD), BF16),
            pltpu.VMEM((L, NY, NZ, PR, HD), BF16),
            pltpu.VMEM((L, NZ, PR, HD), BF16),
            pltpu.VMEM((L, NZ, PR, HD), BF16),
            pltpu.VMEM((L, PR, HD), BF16),
            pltpu.VMEM((NY, 2, PR, HD), BF16),
            sem((7,)), sem((12,)),
            sem((L,)), sem((L,)), sem((L,)), sem((L,)),
            sem((3, 2)), sem((1,)),
            sem((L,)), sem((L,)), sem((L,)), sem((1,)),
        ],
        compiler_params=pltpu.CompilerParams(
            collective_id=0, has_side_effects=True, vmem_limit_bytes=VMEM_LIMIT
        ),
    )(tokens, cotangents, starts, counts, layer_gains, first_map, second_map)


def solution(mesh):
    in_specs = (
        P(None, "dp", None, None),
        P(None, "dp", None, None),
        P(None, "dp", None),
        P(None, "dp"),
        P("pipe", "dp"),
        P("pipe", "dp", None),
        P("pipe", None, "dp"),
    )
    out_specs = (P("pipe", "dp"), P("pipe", "dp", None), P("pipe", None, "dp"))
    return jax.shard_map(
        per_device, mesh=mesh, in_specs=in_specs, out_specs=out_specs, check_vma=False
    )
```

```python
import jax
import jax.numpy as jnp
from jax import lax
from jax.experimental import pallas as pl
from jax.experimental.pallas import tpu as pltpu
from jax.sharding import PartitionSpec as P

MESH = pl.DeviceIdType.MESH
F32 = jnp.float32
BF16 = jnp.bfloat16
L = 8
NX = 4
NZ = 8
NY = 4
HD = 128
T = 64
C = 1024
PR = 40
D = 4096
VMEM_LIMIT = 67043328 - 136 * 1024


def dot(a, b):
    return lax.dot_general(a, b, (((1,), (0,)), ((), ())), preferred_element_type=F32)


def dot_nt(a, b):
    return lax.dot_general(a, b, (((1,), (1,)), ((), ())), preferred_element_type=F32)


def pair_blocks(v):
    zero = jnp.zeros((T, HD), v.dtype)
    top = jnp.concatenate((v[:, :HD], zero), axis=1)
    low = jnp.concatenate((zero, v[:, HD:]), axis=1)
    return jnp.concatenate((top, low), axis=0)


def token_rows(p):
    both = jnp.concatenate((p, p), axis=0)
    high = both.astype(BF16)
    low = (both - high.astype(F32)).astype(BF16)
    return dot_nt(jnp.ones((16, 2 * HD), BF16), jnp.concatenate((high, low), axis=1))[:8]


def to_column(row):
    return jnp.transpose(jnp.broadcast_to(row[0:1], (HD, HD)))[:T]


def twice(v):
    return jnp.concatenate((v, v), axis=1)


def kernel(
    tok, cot, starts, counts, gain_in, first_in, second_in,
    gain_out, first_out, second_out,
    chunk, own_gain, own_first, own_second, wbuf, X, H, M, ES, Fr, R, RR, SS, UU, AA, BS, Q, GP, GX, GF,
    PS, PT, DYP, MK, MKT, G, RA, SA, RB, SB, RC, SD, RD,
    in_sem, sent, s1_recv, z_recv, y_recv, y2_recv, k_recv, tp_recv,
    ga_recv, gy_recv, gz_recv, go_recv,
):
    p = lax.axis_index("pipe")
    d = lax.axis_index("dp")
    x, yh = p // 2, p % 2
    yl, z, c = d // 16, (d // 2) % 8, d % 2
    y = 2 * yh + yl
    k_own = z % 4

    def x_peer(i):
        return (((x + i) % NX) * 2 + yh, d)

    def z_peer(zz):
        return (p, yl * 16 + zz * 2 + c)

    def y_peer(yy):
        return (x * 2 + yy // 2, (yy % 2) * 16 + z * 2 + c)

    core_peer = (p, d + 1 - 2 * c)

    def holder(q):
        yy, h = q // 2, q % 2
        return ((d // 8) * 2 + yy // 2, (yy % 2) * 16 + (2 * k_own + h) * 2 + c)

    def owner(l):
        return (l, 8 * x + 2 * (z // 2) + c)

    def is_me(dev):
        return (dev[0] == p) & (dev[1] == d)

    def arrived(ref, sem):
        pltpu.make_async_copy(ref, ref, sem).wait()

    def remote(src, dst, ss, rs, dev):
        return pltpu.make_async_remote_copy(
            src_ref=src, dst_ref=dst, send_sem=ss, recv_sem=rs, device_id=dev, device_id_type=MESH
        )

    cols = pl.ds(pl.multiple_of(x * C, C), C)
    loads = []
    for b in range(2):
        rows = pl.ds(32 * b, 32)
        loads.append(pltpu.make_async_copy(tok.at[yh, b, :, cols], X.at[0, rows, :], in_sem.at[b]))
        loads.append(pltpu.make_async_copy(cot.at[yh, b, :, cols], M.at[L, rows, :], in_sem.at[2 + b]))
    chunk_loads = [
        pltpu.make_async_copy(first_in, own_first, in_sem.at[4]),
        pltpu.make_async_copy(second_in, own_second, in_sem.at[5]),
        pltpu.make_async_copy(gain_in, own_gain, in_sem.at[6]),
    ]
    for load in chunk_loads + loads:
        load.start()

    barrier = pltpu.get_barrier_semaphore()

    def greet(dev):
        pl.semaphore_signal(barrier, inc=1, device_id=dev, device_id_type=MESH)

    def greet_x(i, carry):
        greet(x_peer(i))
        return carry

    def greet_z(i, carry):
        greet(z_peer((z + i) % NZ))
        return carry

    def greet_y(i, carry):
        greet(y_peer((y + i) % NY))
        return carry

    def greet_far(q, carry):
        for dev in (holder(q), owner(q)):
            @pl.when(jnp.logical_not(is_me(dev)))
            def _():
                greet(dev)
        return carry

    lax.fori_loop(0, 8, greet_far, 0)
    lax.fori_loop(1, NZ, greet_z, 0)
    lax.fori_loop(1, NY, greet_y, 0)
    lax.fori_loop(1, NX, greet_x, 0)
    greet(core_peer)

    row_id = lax.broadcasted_iota(jnp.int32, (T, HD), 0)
    lane_id = lax.broadcasted_iota(jnp.int32, (T, HD), 1) % T

    def documents(index):
        second_mb = index >= 32
        pos = jnp.where(second_mb, index - 32, index)
        doc = jnp.zeros((T, HD), jnp.int32)
        count = jnp.where(second_mb, counts[yh, 1], counts[yh, 0])
        for j in range(4):
            start = jnp.where(second_mb, starts[yh, 1, j], starts[yh, 0, j])
            doc = doc + jnp.where((start <= pos) & (j < count), 1, 0)
        return doc + jnp.where(second_mb, 64, 0)

    same = documents(row_id) == documents(lane_id)
    MK[...] = jnp.where(same & (lane_id <= row_id), 1.0, 0.0)
    MKT[...] = jnp.where(same & (row_id <= lane_id), 1.0, 0.0)
    Fr[L] = jnp.zeros((8, HD), F32)
    BS[L] = jnp.zeros((T, HD), F32)
    half_r = lax.broadcasted_iota(jnp.int32, (HD, HD), 0) // T
    half_l = lax.broadcasted_iota(jnp.int32, (HD, HD), 1) // T
    ones_blocks = jnp.where(half_r == half_l, 1.0, 0.0).astype(BF16)
    head_r = lax.broadcasted_iota(jnp.int32, (2 * HD, HD), 0) // HD
    head_l = lax.broadcasted_iota(jnp.int32, (2 * HD, HD), 1) // T
    ones_heads = jnp.where(head_r == head_l, 1.0, 0.0).astype(BF16)

    me_holder = jnp.int32(0)
    me_owner = jnp.int32(0)
    for q in range(8):
        me_holder = me_holder + jnp.where(is_me(holder(q)), 1, 0)
        me_owner = me_owner + jnp.where(is_me(owner(q)), 1, 0)
    for load in chunk_loads:
        load.wait()
    for q in range(8):
        rows = slice(64 * (q % 2) + 16 * (q // 2), 64 * (q % 2) + 16 * (q // 2) + 16)
        chunk[q, 0:16, :] = own_first[0, rows, :]
        chunk[q, 16:32, :] = own_second[0, rows, :]
        chunk[q, 32:40, :] = jnp.broadcast_to(own_gain[0:1, :].astype(F32), (8, HD)).astype(BF16)
    pl.semaphore_wait(barrier, 30 - me_holder - me_owner)

    def s1_start(q, carry):
        mine = is_me(holder(q))
        slot = wbuf.at[p, c, q // 2, 2 * k_own + q % 2]

        @pl.when(mine)
        def _():
            pltpu.make_async_copy(chunk.at[q], slot, s1_recv.at[p]).start()

        @pl.when(jnp.logical_not(mine))
        def _():
            remote(chunk.at[q], slot, sent.at[0], s1_recv.at[p], holder(q)).start()

        return carry

    lax.fori_loop(0, 8, s1_start, 0)

    def tp_send_all(kind, buf, e, sem):
        slot = buf.at[e, x]
        for i in (2, 1, 3):
            remote(slot, slot, sent.at[kind], sem, x_peer(i)).start()

    def tp_wait(buf, e, sem):
        arrived(buf.at[e, 0 : NX - 1], sem)

    def tp_sum(buf, e):
        total = buf[e, 0].astype(F32)
        for i in range(1, NX):
            total = total + buf[e, i].astype(F32)
        return total

    loads[0].wait()
    loads[2].wait()
    acc = jnp.zeros((T, HD), F32)
    for j in range(C // HD):
        piece = X[0, :, HD * j : HD * j + HD].astype(F32)
        acc = acc + piece * piece
    SS[0, x] = token_rows(acc)
    tp_send_all(2, SS, 0, tp_recv.at[5, 0])

    def spread(l, carry):
        slot = wbuf.at[l, c, y, z]
        arrived(slot, s1_recv.at[l])

        def go(i, inner):
            remote(slot, slot, sent.at[5], z_recv.at[l], z_peer((z + i) % NZ)).start()
            return inner

        return lax.fori_loop(1, NZ, go, carry)

    lax.fori_loop(0, L, spread, 0)

    def along_y(l):
        arrived(wbuf.at[l, c, y, 0 : NZ - 1], z_recv.at[l])
        slot = wbuf.at[l, c, y]
        for i in (1, 3):
            remote(slot, slot, sent.at[6], y_recv.at[l], y_peer((y + i) % NY)).start()

    def along_y_again(l):
        arrived(wbuf.at[l, c, 0:2], y_recv.at[l])
        for i, half in ((1, 0), (3, NZ // 2)):
            slot = wbuf.at[l, c, (y + NY - i) % NY, half : half + NZ // 2]
            remote(slot, slot, sent.at[12], y2_recv.at[l], y_peer((y + i) % NY)).start()

    def to_core(l):
        arrived(wbuf.at[l, c, 0], y2_recv.at[l])
        slot = wbuf.at[l, c]
        remote(slot, slot, sent.at[7], k_recv.at[l], core_peer).start()

    along_y(0)
    along_y_again(0)
    along_y(1)
    to_core(0)
    along_y_again(1)
    along_y(2)

    def w1(l, t):
        return jnp.concatenate(
            [
                wbuf[l, cc, yy, 2 * t + h, 0:16, :]
                for cc in range(2) for h in range(2) for yy in range(NY)
            ],
            axis=0,
        )

    def w2(l, t):
        heads = [
            jnp.concatenate(
                [wbuf[l, cc, yy, 2 * t + h, 16:32, :] for h in range(2) for yy in range(NY)], axis=0
            )
            for cc in range(2)
        ]
        return jnp.concatenate(heads, axis=1)

    def gains(l, t):
        heads = []
        for cc in range(2):
            g8 = wbuf[l, cc, 0, 2 * t, 32:40, :].astype(F32)
            heads.append(jnp.concatenate([g8] * 8, axis=0))
        return jnp.concatenate(heads, axis=1)

    def cols_of(t):
        return slice(256 * t, 256 * t + 256)

    def lanes_of(t):
        return slice(HD * t, HD * t + HD)

    def gram_part(l):
        total = jnp.zeros((HD, HD), F32)
        for t in range(4):
            block = w2(l, t)
            total = total + dot_nt(block, block)
        for i in range(NX):
            GP[l, i] = total[32 * i : 32 * i + 32]
        GX[l, x] = GP[l, x]
        for i in (2, 1, 3):
            dst = (x + i) % NX
            remote(
                GP.at[l, dst], GX.at[l, x], sent.at[13], tp_recv.at[3, l % 2], x_peer(i)
            ).start()

    def gram_sum(l):
        tp_wait(GX, l, tp_recv.at[3, l % 2])
        GF[l, x] = tp_sum(GX, l)
        tp_send_all(14, GF, l, tp_recv.at[4, l % 2])

    arrived(wbuf.at[0, c], k_recv.at[0])
    gram_part(0)

    def forward(l, carry):
        raw = []
        for t in range(4):
            h = (X[l, :, cols_of(t)].astype(F32) * gains(l, t)).astype(BF16)
            H[l, :, cols_of(t)] = h
            raw.append(dot_nt(h, pair_blocks(h)))

        @pl.when(l == 0)
        def _():
            tp_wait(SS, 0, tp_recv.at[5, 0])
            Q[...] = tp_sum(SS, 0)

        @pl.when(l > 0)
        def _():
            below = jnp.maximum(l - 1, 0)
            tp_wait(UU, below, tp_recv.at[1, below % 2])
            tp_wait(GF, below, tp_recv.at[4, below % 2])
            gram = GF[below].reshape(HD, HD)
            high = gram.astype(BF16)
            low = (gram - high.astype(F32)).astype(BF16)
            r = R[below]
            u = tp_sum(UU, below)
            rg = dot(jnp.concatenate((r, r), axis=1), jnp.concatenate((high, low), axis=0))
            BS[l] = u + rg
            Q[...] = Q[...] + token_rows(r.astype(F32) * (2.0 * u + rg))

        f_row = lax.rsqrt(jnp.maximum(Q[...], 0.0) * (1.0 / D) + 1e-05)
        Fr[l] = f_row
        f_key = f_row[0:1]
        scale = to_column(f_row) * f_key * (1.0 / HD)
        mask = MK[...]
        part = jnp.zeros((T, HD), F32)
        for t in range(4):
            e = jnp.exp(raw[t] * scale).astype(BF16)
            ES[l, :, lanes_of(t)] = e
            e = (e.astype(F32) * mask).astype(BF16)
            sums = dot(e, ones_blocks)
            prob = (e.astype(F32) * f_key / sums).astype(BF16)
            mixed = dot(prob, pair_blocks(H[l, :, cols_of(t)])).astype(BF16)
            M[l, :, cols_of(t)] = mixed
            part = part + dot(mixed, w1(l, t))
        RR[l, x] = part.astype(BF16)
        tp_send_all(1, RR, l, tp_recv.at[0, l % 2])

        @pl.when(l < L - 1)
        def _():
            u = jnp.zeros((T, HD), F32)
            for t in range(4):
                u = u + dot_nt(X[l, :, cols_of(t)], w2(l, t))
            UU[l, x] = u.astype(BF16)
            tp_send_all(3, UU, l, tp_recv.at[1, l % 2])

        @pl.when(l == L - 1)
        def _():
            loads[1].wait()
            loads[3].wait()
            acc = jnp.zeros((T, HD), F32)
            for t in range(4):
                acc = acc + dot_nt(M[L, :, cols_of(t)], w2(L - 1, t))
            AA[L - 1, x, 0:64, :] = acc.astype(BF16)
            AA[L - 1, x, 64:80, :] = jnp.zeros((16, HD), BF16)
            tp_send_all(4, AA, L - 1, tp_recv.at[2, (L - 1) % 2])
            DYP[...] = M[L].astype(F32)

        @pl.when(l + 1 < L)
        def _():
            to_core(l + 1)

        @pl.when(l < L - 1)
        def _():
            gram_sum(l)

        @pl.when(l + 2 < L)
        def _():
            along_y_again(l + 2)

        @pl.when(l + 3 < L)
        def _():
            along_y(l + 3)

        @pl.when(l + 1 < L)
        def _():
            arrived(wbuf.at[l + 1, c], k_recv.at[l + 1])

        @pl.when(l + 1 < L - 1)
        def _():
            gram_part(l + 1)

        tp_wait(RR, l, tp_recv.at[0, l % 2])
        r = tp_sum(RR, l).astype(BF16)
        R[l] = r
        for t in range(4):
            X[l + 1, :, cols_of(t)] = (
                X[l, :, cols_of(t)].astype(F32) + dot(r, w2(l, t))
            ).astype(BF16)

        return carry

    lax.fori_loop(0, L, forward, 0)

    def one_layer(l):
        f_row = Fr[l]
        f_key = f_row[0:1]
        f_col = to_column(f_row)
        mask = MK[...]
        mask_t = MKT[...]
        for t in range(4):
            es = ES[l, :, lanes_of(t)].astype(F32)
            e = es * mask
            sums = dot(e.astype(BF16), ones_blocks)
            PS[:, lanes_of(t)] = e / sums
            et = es * mask_t
            PT[:, lanes_of(t)] = et / jnp.sum(et, axis=0, keepdims=True)

        tp_wait(AA, l, tp_recv.at[2, l % 2])
        total = tp_sum(AA, l)
        s_row = total[64:72] + total[72:80]
        f_next = Fr[l + 1]
        coef = to_column(f_next * f_next * f_next * s_row * (1.0 / D))
        dr = total[:64] - coef * BS[l + 1]
        dr_b = dr.astype(BF16)
        coef2 = twice(coef)
        f_col2 = twice(f_col)
        s_part = jnp.zeros((T, HD), F32)
        acc = jnp.zeros((T, HD), F32)
        below = jnp.maximum(l - 1, 0)
        for t in range(4):
            h = H[l, :, cols_of(t)]
            blocks = pair_blocks(h)
            dm = dot_nt(dr_b, w1(l, t)).astype(BF16)
            dm_blocks = pair_blocks(dm)
            prob = PS[:, lanes_of(t)]
            prob_t = PT[:, lanes_of(t)]
            inner = dot(dm * M[l, :, cols_of(t)], ones_heads)
            dp = dot_nt(dm, blocks) * f_key
            dp_t = dot_nt(h, dm_blocks) * f_col
            ds = prob * (dp - inner)
            inner_t = jnp.sum(prob_t * dp_t, axis=0, keepdims=True)
            ds_t = prob_t * (dp_t - inner_t)
            both = (ds + ds_t) * f_key * (1.0 / HD)
            left = jnp.concatenate((both.astype(BF16), prob_t.astype(BF16)), axis=1)
            dn = dot(left, jnp.concatenate((blocks, dm_blocks), axis=0))
            xs = X[l, :, cols_of(t)].astype(F32)
            gdn = dn * gains(l, t)
            dy = DYP[:, cols_of(t)] - X[l + 1, :, cols_of(t)].astype(F32) * coef2
            M[L, :, cols_of(t)] = dy.astype(BF16)
            dyp = dy + gdn * f_col2
            DYP[:, cols_of(t)] = dyp
            acc = acc + dot_nt(dyp.astype(BF16), w2(below, t))
            prod = gdn * xs
            s_part = s_part + prod[:, :HD] + prod[:, HD:]
            dgain = jnp.sum(dn * xs * f_col2, axis=0, keepdims=True)
            wide = jnp.broadcast_to(dgain, (8, 256)).astype(BF16)
            for cc in range(2):
                for h2 in range(2):
                    for yy in range(NY):
                        G[l, cc, yy, 2 * t + h2, 32:40, :] = wide[:, HD * cc : HD * cc + HD]

        @pl.when(l > 0)
        def _():
            s_new = token_rows(s_part)
            s_high = s_new.astype(BF16).astype(F32)
            AA[below, x, 0:64, :] = acc.astype(BF16)
            AA[below, x, 64:80, :] = jnp.concatenate((s_high, s_new - s_high), axis=0).astype(BF16)
            tp_send_all(4, AA, below, tp_recv.at[2, below % 2])

        zeros = jnp.zeros((T, HD), F32)
        dr_t = jnp.transpose(jnp.concatenate((dr, zeros), axis=0)).astype(BF16)[:, :T]
        r_t = jnp.transpose(jnp.concatenate((R[l].astype(F32), zeros), axis=0)).astype(BF16)[:, :T]
        for t in range(4):
            g1 = dot(dr_t, M[l, :, cols_of(t)]).astype(BF16)
            g2 = dot(r_t, M[L, :, cols_of(t)]).astype(BF16)
            for cc in range(2):
                for q in range(8):
                    rows = slice(64 * (q % 2) + 16 * (q // 2), 64 * (q % 2) + 16 * (q // 2) + 16)
                    lanes = slice(HD * cc, HD * cc + HD)
                    G[l, cc, q // 2, 2 * t + q % 2, 0:16, :] = g1[rows, lanes]
                    G[l, cc, q // 2, 2 * t + q % 2, 16:32, :] = g2[rows, lanes]
        remote(G.at[l, 1 - c], RA.at[l], sent.at[8], ga_recv.at[l], core_peer).start()

    def core_sums(l):
        arrived(RA.at[l], ga_recv.at[l])

        def one(i, carry):
            SA[l, i] = (G[l, c, i].astype(F32) + RA[l, i].astype(F32)).astype(BF16)
            return carry

        lax.fori_loop(0, NY, one, 0)
        RB[l, y] = SA[l, y]
        for i in (2, 1, 3):
            yy = (y + i) % NY
            remote(SA.at[l, yy], RB.at[l, y], sent.at[9], gy_recv.at[l], y_peer(yy)).start()

    def y_sums(l):
        arrived(RB.at[l, 0 : NY - 1], gy_recv.at[l])
        total = RB[l, 0].astype(F32)
        for i in range(1, NY):
            total = total + RB[l, i].astype(F32)
        SB[l] = total.astype(BF16)
        RC[l, z] = SB[l, z]

        def go(i, carry):
            zz = (z + i) % NZ
            remote(SB.at[l, zz], RC.at[l, z], sent.at[10], gz_recv.at[l], z_peer(zz)).start()
            return carry

        lax.fori_loop(1, NZ, go, 0)

    def z_sums(l):
        arrived(RC.at[l, 0 : NZ - 1], gz_recv.at[l])
        total = RC[l, 0].astype(F32)
        for i in range(1, NZ):
            total = total + RC[l, i].astype(F32)
        SD[l] = total.astype(BF16)
        mine = is_me(owner(l))

        @pl.when(mine)
        def _():
            pltpu.make_async_copy(SD.at[l], RD.at[y, z % 2], go_recv.at[0]).start()

        @pl.when(jnp.logical_not(mine))
        def _():
            remote(SD.at[l], RD.at[y, z % 2], sent.at[11], go_recv.at[0], owner(l)).start()

    def backward(i, carry):
        @pl.when(i < L)
        def _():
            one_layer(L - 1 - i)

        @pl.when((i >= 1) & (i < L + 1))
        def _():
            core_sums(L - i)

        @pl.when((i >= 2) & (i < L + 2))
        def _():
            y_sums(L + 1 - i)

        @pl.when(i >= 3)
        def _():
            z_sums(L + 2 - i)

        return carry

    lax.fori_loop(0, L + 3, backward, 0)

    arrived(RD, go_recv.at[0])
    grads = []
    for part in range(2):
        rows = slice(16 * part, 16 * part + 16)
        blocks = [RD[yy, h, rows, :].astype(F32) for h in range(2) for yy in range(NY)]
        grads.append(jnp.concatenate(blocks, axis=0))
    first_out[0] = jnp.transpose(grads[0])
    second_out[0] = grads[1]
    gain_out[...] = RD[0, 0, 32:40, :].astype(F32)[0:1]

    for used, sem, pieces in ((me_holder, 0, chunk), (me_owner, 11, SD)):
        @pl.when(used > 0)
        def _():
            arrived(pieces.at[0:7], sent.at[sem])

        @pl.when(used == 0)
        def _():
            arrived(pieces, sent.at[sem])

    arrived(RR.at[0:6], sent.at[1])
    arrived(SS.at[0, 0:3], sent.at[2])
    arrived(UU.at[0:7, 0:3], sent.at[3])
    arrived(AA.at[0:6], sent.at[4])
    arrived(wbuf.at[0:7, 0, 0], sent.at[5])
    arrived(wbuf.at[0:2], sent.at[6])
    arrived(wbuf.at[0:1], sent.at[12])
    arrived(GP.at[0:7, 0:3], sent.at[13])
    arrived(GF.at[0:7, 0:3], sent.at[14])
    arrived(wbuf.at[0:4], sent.at[7])
    arrived(G.at[0:4], sent.at[8])
    arrived(SA.at[0:6], sent.at[9])
    arrived(SB.at[0:7], sent.at[10])


def per_device(tokens, cotangents, starts, counts, layer_gains, first_map, second_map):
    vmem = pl.BlockSpec(memory_space=pltpu.VMEM)
    smem = pl.BlockSpec(memory_space=pltpu.SMEM)
    hbm = pl.BlockSpec(memory_space=pl.ANY)
    sem = pltpu.SemaphoreType.DMA
    return pl.pallas_call(
        kernel,
        out_shape=(
            jax.ShapeDtypeStruct((1, HD), F32),
            jax.ShapeDtypeStruct((1, HD, HD), F32),
            jax.ShapeDtypeStruct((1, HD, HD), F32),
        ),
        in_specs=[hbm, hbm, smem, smem, hbm, hbm, hbm],
        out_specs=(vmem, vmem, vmem),
        scratch_shapes=[
            pltpu.VMEM((8, PR, HD), BF16),
            pltpu.VMEM((1, HD), BF16),
            pltpu.VMEM((1, HD, HD), BF16),
            pltpu.VMEM((1, HD, HD), BF16),
            pltpu.VMEM((L, 2, NY, NZ, PR, HD), BF16),
            pltpu.VMEM((L + 1, T, C), BF16),
            pltpu.VMEM((L, T, C), BF16),
            pltpu.VMEM((L + 1, T, C), BF16),
            pltpu.VMEM((L, T, 4 * HD), BF16),
            pltpu.VMEM((L + 1, 8, HD), F32),
            pltpu.VMEM((L, T, HD), BF16),
            pltpu.VMEM((L, NX, T, HD), BF16),
            pltpu.VMEM((1, NX, 8, HD), F32),
            pltpu.VMEM((L, NX, T, HD), BF16),
            pltpu.VMEM((L, NX, 80, HD), BF16),
            pltpu.VMEM((L + 1, T, HD), F32),
            pltpu.VMEM((8, HD), F32),
            pltpu.VMEM((L, NX, HD // NX, HD), F32),
            pltpu.VMEM((L, NX, HD // NX, HD), F32),
            pltpu.VMEM((L, NX, HD // NX, HD), F32),
            pltpu.VMEM((T, 4 * HD), F32),
            pltpu.VMEM((T, 4 * HD), F32),
            pltpu.VMEM((T, C), F32),
            pltpu.VMEM((T, HD), F32),
            pltpu.VMEM((T, HD), F32),
            pltpu.VMEM((L, 2, NY, NZ, PR, HD), BF16),
            pltpu.VMEM((L, NY, NZ, PR, HD), BF16),
            pltpu.VMEM((L, NY, NZ, PR, HD), BF16),
            pltpu.VMEM((L, NY, NZ, PR, HD), BF16),
            pltpu.VMEM((L, NZ, PR, HD), BF16),
            pltpu.VMEM((L, NZ, PR, HD), BF16),
            pltpu.VMEM((L, PR, HD), BF16),
            pltpu.VMEM((NY, 2, PR, HD), BF16),
            sem((7,)), sem((15,)),
            sem((L,)), sem((L,)), sem((L,)), sem((L,)), sem((L,)),
            sem((6, 2)),
            sem((L,)), sem((L,)), sem((L,)), sem((1,)),
        ],
        compiler_params=pltpu.CompilerParams(
            collective_id=0, has_side_effects=True, vmem_limit_bytes=VMEM_LIMIT
        ),
    )(tokens, cotangents, starts, counts, layer_gains, first_map, second_map)


def solution(mesh):
    in_specs = (
        P(None, "dp", None, None),
        P(None, "dp", None, None),
        P(None, "dp", None),
        P(None, "dp"),
        P("pipe", "dp"),
        P("pipe", "dp", None),
        P("pipe", None, "dp"),
    )
    out_specs = (P("pipe", "dp"), P("pipe", "dp", None), P("pipe", None, "dp"))
    return jax.shard_map(
        per_device, mesh=mesh, in_specs=in_specs, out_specs=out_specs, check_vma=False
    )
```

```python
import jax
import jax.numpy as jnp
from jax import lax
from jax.experimental import pallas as pl
from jax.experimental.pallas import tpu as pltpu
from jax.sharding import PartitionSpec as P

MESH = pl.DeviceIdType.MESH
F32 = jnp.float32
BF16 = jnp.bfloat16
L = 8
NX = 4
NZ = 8
NY = 4
HD = 128
T = 64
C = 1024
PR = 40
D = 4096
VMEM_LIMIT = 67043328 - 136 * 1024


def dot(a, b):
    return lax.dot_general(a, b, (((1,), (0,)), ((), ())), preferred_element_type=F32)


def dot_nt(a, b):
    return lax.dot_general(a, b, (((1,), (1,)), ((), ())), preferred_element_type=F32)


def pair_blocks(v):
    zero = jnp.zeros((T, HD), v.dtype)
    top = jnp.concatenate((v[:, :HD], zero), axis=1)
    low = jnp.concatenate((zero, v[:, HD:]), axis=1)
    return jnp.concatenate((top, low), axis=0)


def token_rows(p):
    both = jnp.concatenate((p, p), axis=0)
    high = both.astype(BF16)
    low = (both - high.astype(F32)).astype(BF16)
    return dot_nt(jnp.ones((16, 2 * HD), BF16), jnp.concatenate((high, low), axis=1))[:8]


def to_column(row):
    return jnp.transpose(jnp.broadcast_to(row[0:1], (HD, HD)))[:T]


def twice(v):
    return jnp.concatenate((v, v), axis=1)


def kernel(
    tok, cot, starts, counts, gain_in, first_in, second_in,
    gain_out, first_out, second_out,
    chunk, own_gain, own_first, own_second, wbuf, X, H, M, ES, Fr, R, RR, SS, UU, AA, BS, Q, GP, GX, GF,
    PS, PT, ZS, YS, DYP, MK, MKT, G, RA, SA, RB, SB, RC, SD, RD,
    in_sem, sent, s1_recv, z_recv, y_recv, y2_recv, k_recv, tp_recv,
    ga_recv, gy_recv, gz_recv, go_recv,
):
    p = lax.axis_index("pipe")
    d = lax.axis_index("dp")
    x, yh = p // 2, p % 2
    yl, z, c = d // 16, (d // 2) % 8, d % 2
    y = 2 * yh + yl
    k_own = z % 4

    def x_peer(i):
        return (((x + i) % NX) * 2 + yh, d)

    def z_peer(zz):
        return (p, yl * 16 + zz * 2 + c)

    def y_peer(yy):
        return (x * 2 + yy // 2, (yy % 2) * 16 + z * 2 + c)

    core_peer = (p, d + 1 - 2 * c)

    def holder(q):
        yy, h = q // 2, q % 2
        return ((d // 8) * 2 + yy // 2, (yy % 2) * 16 + (2 * k_own + h) * 2 + c)

    def owner(l):
        return (l, 8 * x + 2 * (z // 2) + c)

    def is_me(dev):
        return (dev[0] == p) & (dev[1] == d)

    def arrived(ref, sem):
        pltpu.make_async_copy(ref, ref, sem).wait()

    def remote(src, dst, ss, rs, dev):
        return pltpu.make_async_remote_copy(
            src_ref=src, dst_ref=dst, send_sem=ss, recv_sem=rs, device_id=dev, device_id_type=MESH
        )

    cols = pl.ds(pl.multiple_of(x * C, C), C)
    loads = []
    for b in range(2):
        rows = pl.ds(32 * b, 32)
        loads.append(pltpu.make_async_copy(tok.at[yh, b, :, cols], X.at[0, rows, :], in_sem.at[b]))
        loads.append(pltpu.make_async_copy(cot.at[yh, b, :, cols], M.at[L, rows, :], in_sem.at[2 + b]))
    chunk_loads = [
        pltpu.make_async_copy(first_in, own_first, in_sem.at[4]),
        pltpu.make_async_copy(second_in, own_second, in_sem.at[5]),
        pltpu.make_async_copy(gain_in, own_gain, in_sem.at[6]),
    ]
    for load in chunk_loads + loads:
        load.start()

    barrier = pltpu.get_barrier_semaphore()

    def greet(dev):
        pl.semaphore_signal(barrier, inc=1, device_id=dev, device_id_type=MESH)

    def greet_x(i, carry):
        greet(x_peer(i))
        return carry

    def greet_z(i, carry):
        greet(z_peer((z + i) % NZ))
        return carry

    def greet_y(i, carry):
        greet(y_peer((y + i) % NY))
        return carry

    def greet_far(q, carry):
        for dev in (holder(q), owner(q)):
            @pl.when(jnp.logical_not(is_me(dev)))
            def _():
                greet(dev)
        return carry

    lax.fori_loop(0, 8, greet_far, 0)
    lax.fori_loop(1, NZ, greet_z, 0)
    lax.fori_loop(1, NY, greet_y, 0)
    lax.fori_loop(1, NX, greet_x, 0)
    greet(core_peer)

    row_id = lax.broadcasted_iota(jnp.int32, (T, HD), 0)
    lane_id = lax.broadcasted_iota(jnp.int32, (T, HD), 1) % T

    def documents(index):
        second_mb = index >= 32
        pos = jnp.where(second_mb, index - 32, index)
        doc = jnp.zeros((T, HD), jnp.int32)
        count = jnp.where(second_mb, counts[yh, 1], counts[yh, 0])
        for j in range(4):
            start = jnp.where(second_mb, starts[yh, 1, j], starts[yh, 0, j])
            doc = doc + jnp.where((start <= pos) & (j < count), 1, 0)
        return doc + jnp.where(second_mb, 64, 0)

    same = documents(row_id) == documents(lane_id)
    MK[...] = jnp.where(same & (lane_id <= row_id), 1.0, 0.0)
    MKT[...] = jnp.where(same & (row_id <= lane_id), 1.0, 0.0)
    Fr[L] = jnp.zeros((8, HD), F32)
    BS[L] = jnp.zeros((T, HD), F32)
    half_r = lax.broadcasted_iota(jnp.int32, (HD, HD), 0) // T
    half_l = lax.broadcasted_iota(jnp.int32, (HD, HD), 1) // T
    ones_blocks = jnp.where(half_r == half_l, 1.0, 0.0).astype(BF16)
    wide_r = lax.broadcasted_iota(jnp.int32, (HD, 2 * HD), 0) // T
    wide_l = lax.broadcasted_iota(jnp.int32, (HD, 2 * HD), 1) // HD
    ones_wide = jnp.where(wide_r == wide_l, 1.0, 0.0).astype(BF16)
    head_r = lax.broadcasted_iota(jnp.int32, (2 * HD, HD), 0) // HD
    head_l = lax.broadcasted_iota(jnp.int32, (2 * HD, HD), 1) // T
    ones_heads = jnp.where(head_r == head_l, 1.0, 0.0).astype(BF16)

    me_holder = jnp.int32(0)
    me_owner = jnp.int32(0)
    for q in range(8):
        me_holder = me_holder + jnp.where(is_me(holder(q)), 1, 0)
        me_owner = me_owner + jnp.where(is_me(owner(q)), 1, 0)
    for load in chunk_loads:
        load.wait()
    for q in range(8):
        rows = slice(64 * (q % 2) + 16 * (q // 2), 64 * (q % 2) + 16 * (q // 2) + 16)
        chunk[q, 0:16, :] = own_first[0, rows, :]
        chunk[q, 16:32, :] = own_second[0, rows, :]
        chunk[q, 32:40, :] = jnp.broadcast_to(own_gain[0:1, :].astype(F32), (8, HD)).astype(BF16)
    pl.semaphore_wait(barrier, 30 - me_holder - me_owner)

    def s1_start(q, carry):
        mine = is_me(holder(q))
        slot = wbuf.at[p, c, q // 2, 2 * k_own + q % 2]

        @pl.when(mine)
        def _():
            pltpu.make_async_copy(chunk.at[q], slot, s1_recv.at[p]).start()

        @pl.when(jnp.logical_not(mine))
        def _():
            remote(chunk.at[q], slot, sent.at[0], s1_recv.at[p], holder(q)).start()

        return carry

    lax.fori_loop(0, 8, s1_start, 0)

    def tp_send_all(kind, buf, e, sem):
        slot = buf.at[e, x]
        for i in (2, 1, 3):
            remote(slot, slot, sent.at[kind], sem, x_peer(i)).start()

    def tp_wait(buf, e, sem):
        arrived(buf.at[e, 0 : NX - 1], sem)

    def tp_sum(buf, e):
        total = buf[e, 0].astype(F32)
        for i in range(1, NX):
            total = total + buf[e, i].astype(F32)
        return total

    loads[0].wait()
    loads[2].wait()
    acc = jnp.zeros((T, HD), F32)
    for j in range(C // HD):
        piece = X[0, :, HD * j : HD * j + HD].astype(F32)
        acc = acc + piece * piece
    SS[0, x] = token_rows(acc)
    tp_send_all(2, SS, 0, tp_recv.at[5, 0])

    def spread(l, carry):
        slot = wbuf.at[l, c, y, z]
        arrived(slot, s1_recv.at[l])

        def go(i, inner):
            remote(slot, slot, sent.at[5], z_recv.at[l], z_peer((z + i) % NZ)).start()
            return inner

        return lax.fori_loop(1, NZ, go, carry)

    lax.fori_loop(0, L, spread, 0)

    def along_y(l):
        arrived(wbuf.at[l, c, y, 0 : NZ - 1], z_recv.at[l])
        slot = wbuf.at[l, c, y]
        for i in (1, 3):
            remote(slot, slot, sent.at[6], y_recv.at[l], y_peer((y + i) % NY)).start()

    def along_y_again(l):
        arrived(wbuf.at[l, c, 0:2], y_recv.at[l])
        for i, half in ((1, 0), (3, NZ // 2)):
            slot = wbuf.at[l, c, (y + NY - i) % NY, half : half + NZ // 2]
            remote(slot, slot, sent.at[12], y2_recv.at[l], y_peer((y + i) % NY)).start()

    def to_core(l):
        arrived(wbuf.at[l, c, 0], y2_recv.at[l])
        slot = wbuf.at[l, c]
        remote(slot, slot, sent.at[7], k_recv.at[l], core_peer).start()

    along_y(0)
    along_y(1)
    along_y_again(0)
    along_y(2)
    along_y_again(1)
    to_core(0)
    along_y(3)
    along_y_again(2)
    to_core(1)

    def w1(l, t):
        return jnp.concatenate(
            [
                wbuf[l, cc, yy, 2 * t + h, 0:16, :]
                for cc in range(2) for h in range(2) for yy in range(NY)
            ],
            axis=0,
        )

    def w2(l, t):
        heads = [
            jnp.concatenate(
                [wbuf[l, cc, yy, 2 * t + h, 16:32, :] for h in range(2) for yy in range(NY)], axis=0
            )
            for cc in range(2)
        ]
        return jnp.concatenate(heads, axis=1)

    def gains(l, t):
        heads = []
        for cc in range(2):
            g8 = wbuf[l, cc, 0, 2 * t, 32:40, :].astype(F32)
            heads.append(jnp.concatenate([g8] * 8, axis=0))
        return jnp.concatenate(heads, axis=1)

    def cols_of(t):
        return slice(256 * t, 256 * t + 256)

    def lanes_of(t):
        return slice(HD * t, HD * t + HD)

    def gram_part(l):
        total = jnp.zeros((HD, HD), F32)
        for t in range(4):
            block = w2(l, t)
            total = total + dot_nt(block, block)
        for i in range(NX):
            GP[l, i] = total[32 * i : 32 * i + 32]
        GX[l, x] = GP[l, x]
        for i in (2, 1, 3):
            dst = (x + i) % NX
            remote(
                GP.at[l, dst], GX.at[l, x], sent.at[13], tp_recv.at[3, l % 2], x_peer(i)
            ).start()

    def gram_sum(l):
        tp_wait(GX, l, tp_recv.at[3, l % 2])
        GF[l, x] = tp_sum(GX, l)
        tp_send_all(14, GF, l, tp_recv.at[4, l % 2])

    arrived(wbuf.at[0, c], k_recv.at[0])
    gram_part(0)

    def forward(l, carry):
        raw = []
        for t in range(4):
            h = (X[l, :, cols_of(t)].astype(F32) * gains(l, t)).astype(BF16)
            H[l, :, cols_of(t)] = h
            raw.append(dot_nt(h, pair_blocks(h)))

        @pl.when(l < L - 1)
        def _():
            u = jnp.zeros((T, HD), F32)
            for t in range(4):
                u = u + dot_nt(X[l, :, cols_of(t)], w2(l, t))
            UU[l, x] = u.astype(BF16)
            tp_send_all(3, UU, l, tp_recv.at[1, l % 2])

        @pl.when(l == 0)
        def _():
            tp_wait(SS, 0, tp_recv.at[5, 0])
            Q[...] = tp_sum(SS, 0)

        @pl.when(l > 0)
        def _():
            below = jnp.maximum(l - 1, 0)
            tp_wait(UU, below, tp_recv.at[1, below % 2])
            tp_wait(GF, below, tp_recv.at[4, below % 2])
            gram = GF[below].reshape(HD, HD)
            high = gram.astype(BF16)
            low = (gram - high.astype(F32)).astype(BF16)
            r = R[below]
            u = tp_sum(UU, below)
            rg = dot(jnp.concatenate((r, r), axis=1), jnp.concatenate((high, low), axis=0))
            BS[l] = u + rg
            Q[...] = Q[...] + token_rows(r.astype(F32) * (2.0 * u + rg))

        f_row = lax.rsqrt(jnp.maximum(Q[...], 0.0) * (1.0 / D) + 1e-05)
        Fr[l] = f_row
        f_key = f_row[0:1]
        scale = to_column(f_row) * f_key * (1.0 / HD)
        mask = MK[...]
        part = jnp.zeros((T, HD), F32)
        for t in range(4):
            e = jnp.exp(raw[t] * scale).astype(BF16)
            ES[l, :, lanes_of(t)] = e
            e = (e.astype(F32) * mask).astype(BF16)
            sums = dot(e, ones_wide)
            weighted = dot((e.astype(F32) * f_key).astype(BF16), pair_blocks(H[l, :, cols_of(t)]))
            mixed = (weighted / sums).astype(BF16)
            M[l, :, cols_of(t)] = mixed
            part = part + dot(mixed, w1(l, t))
        RR[l, x] = part.astype(BF16)
        tp_send_all(1, RR, l, tp_recv.at[0, l % 2])

        @pl.when(l == L - 1)
        def _():
            loads[1].wait()
            loads[3].wait()
            acc = jnp.zeros((T, HD), F32)
            for t in range(4):
                acc = acc + dot_nt(M[L, :, cols_of(t)], w2(L - 1, t))
            AA[L - 1, x, 0:64, :] = acc.astype(BF16)
            AA[L - 1, x, 64:80, :] = jnp.zeros((16, HD), BF16)
            tp_send_all(4, AA, L - 1, tp_recv.at[2, (L - 1) % 2])
            DYP[...] = M[L].astype(F32)

        @pl.when(l < L - 1)
        def _():
            gram_sum(l)

        @pl.when(l + 2 < L)
        def _():
            to_core(l + 2)

        @pl.when(l + 3 < L)
        def _():
            along_y_again(l + 3)

        @pl.when(l + 4 < L)
        def _():
            along_y(l + 4)

        @pl.when(l + 1 < L)
        def _():
            arrived(wbuf.at[l + 1, c], k_recv.at[l + 1])

        @pl.when(l + 1 < L - 1)
        def _():
            gram_part(l + 1)

        tp_wait(RR, l, tp_recv.at[0, l % 2])
        r = tp_sum(RR, l).astype(BF16)
        R[l] = r
        for t in range(4):
            X[l + 1, :, cols_of(t)] = (
                X[l, :, cols_of(t)].astype(F32) + dot(r, w2(l, t))
            ).astype(BF16)

        return carry

    lax.fori_loop(0, L, forward, 0)

    def one_layer(l):
        f_row = Fr[l]
        f_key = f_row[0:1]
        f_col = to_column(f_row)
        mask = MK[...]
        mask_t = MKT[...]
        for t in range(4):
            es = ES[l, :, lanes_of(t)].astype(F32)
            e = es * mask
            sums = dot(e.astype(BF16), ones_blocks)
            PS[:, lanes_of(t)] = e / sums
            et = es * mask_t
            PT[:, lanes_of(t)] = et / jnp.sum(et, axis=0, keepdims=True)
            weight = w1(l, t)
            for src, dst in ((H, ZS), (M, YS)):
                pair = src[l, :, cols_of(t)]
                products = [
                    dot(pair[:, :HD], weight[:HD]), dot(pair[:, HD:], weight[HD:])
                ]
                dst[:, cols_of(t)] = jnp.concatenate(products, axis=1).astype(BF16)

        tp_wait(AA, l, tp_recv.at[2, l % 2])
        total = tp_sum(AA, l)
        s_row = total[64:72] + total[72:80]
        f_next = Fr[l + 1]
        coef = to_column(f_next * f_next * f_next * s_row * (1.0 / D))
        dr = total[:64] - coef * BS[l + 1]
        dr_b = dr.astype(BF16)
        dr_blocks = pair_blocks(twice(dr_b))
        dr2 = twice(dr)
        coef2 = twice(coef)
        f_col2 = twice(f_col)
        s_part = jnp.zeros((T, HD), F32)
        acc = jnp.zeros((T, HD), F32)
        below = jnp.maximum(l - 1, 0)
        for t in range(4):
            h = H[l, :, cols_of(t)]
            blocks = pair_blocks(h)
            dm = dot_nt(dr_b, w1(l, t)).astype(BF16)
            dm_blocks = pair_blocks(dm)
            prob = PS[:, lanes_of(t)]
            prob_t = PT[:, lanes_of(t)]
            zs = ZS[:, cols_of(t)]
            inner = dot((dr2 * YS[:, cols_of(t)].astype(F32)).astype(BF16), ones_heads)
            dp = dot_nt(dr_b, jnp.concatenate((zs[:, :HD], zs[:, HD:]), axis=0)) * f_key
            dp_t = dot_nt(zs, dr_blocks) * f_col
            ds = prob * (dp - inner)
            inner_t = jnp.sum(prob_t * dp_t, axis=0, keepdims=True)
            ds_t = prob_t * (dp_t - inner_t)
            both = (ds + ds_t) * f_key * (1.0 / HD)
            left = jnp.concatenate((both.astype(BF16), prob_t.astype(BF16)), axis=1)
            dn = dot(left, jnp.concatenate((blocks, dm_blocks), axis=0))
            xs = X[l, :, cols_of(t)].astype(F32)
            gdn = dn * gains(l, t)
            dy = DYP[:, cols_of(t)] - X[l + 1, :, cols_of(t)].astype(F32) * coef2
            M[L, :, cols_of(t)] = dy.astype(BF16)
            dyp = dy + gdn * f_col2
            DYP[:, cols_of(t)] = dyp
            acc = acc + dot_nt(dyp.astype(BF16), w2(below, t))
            prod = gdn * xs
            s_part = s_part + prod[:, :HD] + prod[:, HD:]
            dgain = jnp.sum(dn * xs * f_col2, axis=0, keepdims=True)
            wide = jnp.broadcast_to(dgain, (8, 256)).astype(BF16)
            for cc in range(2):
                for h2 in range(2):
                    for yy in range(NY):
                        G[l, cc, yy, 2 * t + h2, 32:40, :] = wide[:, HD * cc : HD * cc + HD]

        @pl.when(l > 0)
        def _():
            s_new = token_rows(s_part)
            s_high = s_new.astype(BF16).astype(F32)
            AA[below, x, 0:64, :] = acc.astype(BF16)
            AA[below, x, 64:80, :] = jnp.concatenate((s_high, s_new - s_high), axis=0).astype(BF16)
            tp_send_all(4, AA, below, tp_recv.at[2, below % 2])

        zeros = jnp.zeros((T, HD), F32)
        dr_t = jnp.transpose(jnp.concatenate((dr, zeros), axis=0)).astype(BF16)[:, :T]
        r_t = jnp.transpose(jnp.concatenate((R[l].astype(F32), zeros), axis=0)).astype(BF16)[:, :T]
        for t in range(4):
            g1 = dot(dr_t, M[l, :, cols_of(t)]).astype(BF16)
            g2 = dot(r_t, M[L, :, cols_of(t)]).astype(BF16)
            for cc in range(2):
                for q in range(8):
                    rows = slice(64 * (q % 2) + 16 * (q // 2), 64 * (q % 2) + 16 * (q // 2) + 16)
                    lanes = slice(HD * cc, HD * cc + HD)
                    G[l, cc, q // 2, 2 * t + q % 2, 0:16, :] = g1[rows, lanes]
                    G[l, cc, q // 2, 2 * t + q % 2, 16:32, :] = g2[rows, lanes]
        remote(G.at[l, 1 - c], RA.at[l], sent.at[8], ga_recv.at[l], core_peer).start()

    def core_sums(l):
        arrived(RA.at[l], ga_recv.at[l])

        def one(i, carry):
            SA[l, i] = (G[l, c, i].astype(F32) + RA[l, i].astype(F32)).astype(BF16)
            return carry

        lax.fori_loop(0, NY, one, 0)
        RB[l, y] = SA[l, y]
        for i in (2, 1, 3):
            yy = (y + i) % NY
            remote(SA.at[l, yy], RB.at[l, y], sent.at[9], gy_recv.at[l], y_peer(yy)).start()

    def y_sums(l):
        arrived(RB.at[l, 0 : NY - 1], gy_recv.at[l])
        total = RB[l, 0].astype(F32)
        for i in range(1, NY):
            total = total + RB[l, i].astype(F32)
        SB[l] = total.astype(BF16)
        RC[l, z] = SB[l, z]

        def go(i, carry):
            zz = (z + i) % NZ
            remote(SB.at[l, zz], RC.at[l, z], sent.at[10], gz_recv.at[l], z_peer(zz)).start()
            return carry

        lax.fori_loop(1, NZ, go, 0)

    def z_sums(l):
        arrived(RC.at[l, 0 : NZ - 1], gz_recv.at[l])
        total = RC[l, 0].astype(F32)
        for i in range(1, NZ):
            total = total + RC[l, i].astype(F32)
        SD[l] = total.astype(BF16)
        mine = is_me(owner(l))

        @pl.when(mine)
        def _():
            pltpu.make_async_copy(SD.at[l], RD.at[y, z % 2], go_recv.at[0]).start()

        @pl.when(jnp.logical_not(mine))
        def _():
            remote(SD.at[l], RD.at[y, z % 2], sent.at[11], go_recv.at[0], owner(l)).start()

    def backward(i, carry):
        @pl.when(i < L)
        def _():
            one_layer(L - 1 - i)

        @pl.when((i >= 1) & (i < L + 1))
        def _():
            core_sums(L - i)

        @pl.when((i >= 2) & (i < L + 2))
        def _():
            y_sums(L + 1 - i)

        @pl.when(i >= 3)
        def _():
            z_sums(L + 2 - i)

        return carry

    lax.fori_loop(0, L + 3, backward, 0)

    arrived(RD, go_recv.at[0])
    grads = []
    for part in range(2):
        rows = slice(16 * part, 16 * part + 16)
        blocks = [RD[yy, h, rows, :].astype(F32) for h in range(2) for yy in range(NY)]
        grads.append(jnp.concatenate(blocks, axis=0))
    first_out[0] = jnp.transpose(grads[0])
    second_out[0] = grads[1]
    gain_out[...] = RD[0, 0, 32:40, :].astype(F32)[0:1]

    for used, sem, pieces in ((me_holder, 0, chunk), (me_owner, 11, SD)):
        @pl.when(used > 0)
        def _():
            arrived(pieces.at[0:7], sent.at[sem])

        @pl.when(used == 0)
        def _():
            arrived(pieces, sent.at[sem])

    arrived(RR.at[0:6], sent.at[1])
    arrived(SS.at[0, 0:3], sent.at[2])
    arrived(UU.at[0:7, 0:3], sent.at[3])
    arrived(AA.at[0:6], sent.at[4])
    arrived(wbuf.at[0:7, 0, 0], sent.at[5])
    arrived(wbuf.at[0:2], sent.at[6])
    arrived(wbuf.at[0:1], sent.at[12])
    arrived(GP.at[0:7, 0:3], sent.at[13])
    arrived(GF.at[0:7, 0:3], sent.at[14])
    arrived(wbuf.at[0:4], sent.at[7])
    arrived(G.at[0:4], sent.at[8])
    arrived(SA.at[0:6], sent.at[9])
    arrived(SB.at[0:7], sent.at[10])


def per_device(tokens, cotangents, starts, counts, layer_gains, first_map, second_map):
    vmem = pl.BlockSpec(memory_space=pltpu.VMEM)
    smem = pl.BlockSpec(memory_space=pltpu.SMEM)
    hbm = pl.BlockSpec(memory_space=pltpu.HBM)
    sem = pltpu.SemaphoreType.DMA
    return pl.pallas_call(
        kernel,
        out_shape=(
            jax.ShapeDtypeStruct((1, HD), F32),
            jax.ShapeDtypeStruct((1, HD, HD), F32),
            jax.ShapeDtypeStruct((1, HD, HD), F32),
        ),
        in_specs=[hbm, hbm, smem, smem, hbm, hbm, hbm],
        out_specs=(vmem, vmem, vmem),
        scratch_shapes=[
            pltpu.VMEM((8, PR, HD), BF16),
            pltpu.VMEM((1, HD), BF16),
            pltpu.VMEM((1, HD, HD), BF16),
            pltpu.VMEM((1, HD, HD), BF16),
            pltpu.VMEM((L, 2, NY, NZ, PR, HD), BF16),
            pltpu.VMEM((L + 1, T, C), BF16),
            pltpu.VMEM((L, T, C), BF16),
            pltpu.VMEM((L + 1, T, C), BF16),
            pltpu.VMEM((L, T, 4 * HD), BF16),
            pltpu.VMEM((L + 1, 8, HD), F32),
            pltpu.VMEM((L, T, HD), BF16),
            pltpu.VMEM((L, NX, T, HD), BF16),
            pltpu.VMEM((1, NX, 8, HD), F32),
            pltpu.VMEM((L, NX, T, HD), BF16),
            pltpu.VMEM((L, NX, 80, HD), BF16),
            pltpu.VMEM((L + 1, T, HD), F32),
            pltpu.VMEM((8, HD), F32),
            pltpu.VMEM((L, NX, HD // NX, HD), F32),
            pltpu.VMEM((L, NX, HD // NX, HD), F32),
            pltpu.VMEM((L, NX, HD // NX, HD), F32),
            pltpu.VMEM((T, 4 * HD), F32),
            pltpu.VMEM((T, 4 * HD), F32),
            pltpu.VMEM((T, C), BF16),
            pltpu.VMEM((T, C), BF16),
            pltpu.VMEM((T, C), F32),
            pltpu.VMEM((T, HD), F32),
            pltpu.VMEM((T, HD), F32),
            pltpu.VMEM((L, 2, NY, NZ, PR, HD), BF16),
            pltpu.VMEM((L, NY, NZ, PR, HD), BF16),
            pltpu.VMEM((L, NY, NZ, PR, HD), BF16),
            pltpu.VMEM((L, NY, NZ, PR, HD), BF16),
            pltpu.VMEM((L, NZ, PR, HD), BF16),
            pltpu.VMEM((L, NZ, PR, HD), BF16),
            pltpu.VMEM((L, PR, HD), BF16),
            pltpu.VMEM((NY, 2, PR, HD), BF16),
            sem((7,)), sem((15,)),
            sem((L,)), sem((L,)), sem((L,)), sem((L,)), sem((L,)),
            sem((6, 2)),
            sem((L,)), sem((L,)), sem((L,)), sem((1,)),
        ],
        compiler_params=pltpu.CompilerParams(
            collective_id=0, has_side_effects=True, vmem_limit_bytes=VMEM_LIMIT
        ),
    )(tokens, cotangents, starts, counts, layer_gains, first_map, second_map)


def solution(mesh):
    in_specs = (
        P(None, "dp", None, None),
        P(None, "dp", None, None),
        P(None, "dp", None),
        P(None, "dp"),
        P("pipe", "dp"),
        P("pipe", "dp", None),
        P("pipe", None, "dp"),
    )
    out_specs = (P("pipe", "dp"), P("pipe", "dp", None), P("pipe", None, "dp"))
    return jax.shard_map(
        per_device, mesh=mesh, in_specs=in_specs, out_specs=out_specs, check_vma=False
    )
```

```python
import jax
import jax.numpy as jnp
from jax import lax
from jax.experimental import pallas as pl
from jax.experimental.pallas import tpu as pltpu
from jax.sharding import PartitionSpec as P

MESH = pl.DeviceIdType.MESH
F32 = jnp.float32
BF16 = jnp.bfloat16
L = 8
NX = 4
NZ = 8
NY = 4
HD = 128
T = 64
C = 1024
PR = 40
D = 4096
VMEM_LIMIT = 67043328 - 136 * 1024


def dot(a, b):
    return lax.dot_general(a, b, (((1,), (0,)), ((), ())), preferred_element_type=F32)


def dot_nt(a, b):
    return lax.dot_general(a, b, (((1,), (1,)), ((), ())), preferred_element_type=F32)


def pair_blocks(v):
    zero = jnp.zeros((T, HD), v.dtype)
    top = jnp.concatenate((v[:, :HD], zero), axis=1)
    low = jnp.concatenate((zero, v[:, HD:]), axis=1)
    return jnp.concatenate((top, low), axis=0)


def token_rows(p):
    both = jnp.concatenate((p, p), axis=0)
    high = both.astype(BF16)
    low = (both - high.astype(F32)).astype(BF16)
    return dot_nt(jnp.ones((16, 2 * HD), BF16), jnp.concatenate((high, low), axis=1))[:8]


def to_column(row):
    return jnp.transpose(jnp.broadcast_to(row[0:1], (HD, HD)))[:T]


def twice(v):
    return jnp.concatenate((v, v), axis=1)


def kernel(
    tok, cot, starts, counts, gain_in, first_in, second_in,
    gain_out, first_out, second_out,
    chunk, own_gain, own_first, own_second, wbuf, X, H, M, ES, Fr, R, RR, SS, UU, AA, BS, Q, GP, GX, GF,
    PS, PT, ZS, YS, DYP, MK, MKT, G, RA, SA, RB, SB, RC, SD, RD,
    in_sem, sent, s1_recv, z_recv, y_recv, y2_recv, k_recv, tp_recv,
    ga_recv, gy_recv, gz_recv, go_recv,
):
    p = lax.axis_index("pipe")
    d = lax.axis_index("dp")
    x, yh = p // 2, p % 2
    yl, z, c = d // 16, (d // 2) % 8, d % 2
    y = 2 * yh + yl
    k_own = z % 4

    def x_peer(i):
        return (((x + i) % NX) * 2 + yh, d)

    def z_peer(zz):
        return (p, yl * 16 + zz * 2 + c)

    def y_peer(yy):
        return (x * 2 + yy // 2, (yy % 2) * 16 + z * 2 + c)

    core_peer = (p, d + 1 - 2 * c)

    def holder(q):
        yy, h = q // 2, q % 2
        return ((d // 8) * 2 + yy // 2, (yy % 2) * 16 + (2 * k_own + h) * 2 + c)

    def owner(l):
        return (l, 8 * x + 2 * (z // 2) + c)

    def is_me(dev):
        return (dev[0] == p) & (dev[1] == d)

    def arrived(ref, sem):
        pltpu.make_async_copy(ref, ref, sem).wait()

    def remote(src, dst, ss, rs, dev):
        return pltpu.make_async_remote_copy(
            src_ref=src, dst_ref=dst, send_sem=ss, recv_sem=rs, device_id=dev, device_id_type=MESH
        )

    cols = pl.ds(pl.multiple_of(x * C, C), C)
    loads = []
    for b in range(2):
        rows = pl.ds(32 * b, 32)
        loads.append(pltpu.make_async_copy(tok.at[yh, b, :, cols], X.at[0, rows, :], in_sem.at[b]))
        loads.append(pltpu.make_async_copy(cot.at[yh, b, :, cols], M.at[L, rows, :], in_sem.at[2 + b]))
    chunk_loads = [
        pltpu.make_async_copy(first_in, own_first, in_sem.at[4]),
        pltpu.make_async_copy(second_in, own_second, in_sem.at[5]),
        pltpu.make_async_copy(gain_in, own_gain, in_sem.at[6]),
    ]
    for load in chunk_loads + loads:
        load.start()

    barrier = pltpu.get_barrier_semaphore()

    def greet(dev):
        pl.semaphore_signal(barrier, inc=1, device_id=dev, device_id_type=MESH)

    def greet_x(i, carry):
        greet(x_peer(i))
        return carry

    def greet_z(i, carry):
        greet(z_peer((z + i) % NZ))
        return carry

    def greet_y(i, carry):
        greet(y_peer((y + i) % NY))
        return carry

    def greet_far(q, carry):
        for dev in (holder(q), owner(q)):
            @pl.when(jnp.logical_not(is_me(dev)))
            def _():
                greet(dev)
        return carry

    lax.fori_loop(0, 8, greet_far, 0)
    lax.fori_loop(1, NZ, greet_z, 0)
    lax.fori_loop(1, NY, greet_y, 0)
    lax.fori_loop(1, NX, greet_x, 0)
    greet(core_peer)

    row_id = lax.broadcasted_iota(jnp.int32, (T, HD), 0)
    lane_id = lax.broadcasted_iota(jnp.int32, (T, HD), 1) % T

    def documents(index):
        second_mb = index >= 32
        pos = jnp.where(second_mb, index - 32, index)
        doc = jnp.zeros((T, HD), jnp.int32)
        count = jnp.where(second_mb, counts[yh, 1], counts[yh, 0])
        for j in range(4):
            start = jnp.where(second_mb, starts[yh, 1, j], starts[yh, 0, j])
            doc = doc + jnp.where((start <= pos) & (j < count), 1, 0)
        return doc + jnp.where(second_mb, 64, 0)

    same = documents(row_id) == documents(lane_id)
    MK[...] = jnp.where(same & (lane_id <= row_id), 1.0, 0.0)
    MKT[...] = jnp.where(same & (row_id <= lane_id), 1.0, 0.0)
    Fr[L] = jnp.zeros((8, HD), F32)
    BS[L] = jnp.zeros((T, HD), F32)
    X[L] = jnp.zeros((T, C), BF16)
    half_r = lax.broadcasted_iota(jnp.int32, (HD, HD), 0) // T
    half_l = lax.broadcasted_iota(jnp.int32, (HD, HD), 1) // T
    ones_blocks = jnp.where(half_r == half_l, 1.0, 0.0).astype(BF16)
    wide_r = lax.broadcasted_iota(jnp.int32, (HD, 2 * HD), 0) // T
    wide_l = lax.broadcasted_iota(jnp.int32, (HD, 2 * HD), 1) // HD
    ones_wide = jnp.where(wide_r == wide_l, 1.0, 0.0).astype(BF16)
    head_r = lax.broadcasted_iota(jnp.int32, (2 * HD, HD), 0) // HD
    head_l = lax.broadcasted_iota(jnp.int32, (2 * HD, HD), 1) // T
    ones_heads = jnp.where(head_r == head_l, 1.0, 0.0).astype(BF16)

    me_holder = jnp.int32(0)
    me_owner = jnp.int32(0)
    for q in range(8):
        me_holder = me_holder + jnp.where(is_me(holder(q)), 1, 0)
        me_owner = me_owner + jnp.where(is_me(owner(q)), 1, 0)
    for load in chunk_loads:
        load.wait()
    for q in range(8):
        rows = slice(64 * (q % 2) + 16 * (q // 2), 64 * (q % 2) + 16 * (q // 2) + 16)
        chunk[q, 0:16, :] = own_first[0, rows, :]
        chunk[q, 16:32, :] = own_second[0, rows, :]
        chunk[q, 32:40, :] = jnp.broadcast_to(own_gain[0:1, :].astype(F32), (8, HD)).astype(BF16)
    pl.semaphore_wait(barrier, 30 - me_holder - me_owner)

    def s1_start(q, carry):
        mine = is_me(holder(q))
        slot = wbuf.at[p, c, q // 2, 2 * k_own + q % 2]

        @pl.when(mine)
        def _():
            pltpu.make_async_copy(chunk.at[q], slot, s1_recv.at[p]).start()

        @pl.when(jnp.logical_not(mine))
        def _():
            remote(chunk.at[q], slot, sent.at[0], s1_recv.at[p], holder(q)).start()

        return carry

    lax.fori_loop(0, 8, s1_start, 0)

    def tp_send_all(kind, buf, e, sem):
        slot = buf.at[e, x]
        for i in (2, 1, 3):
            remote(slot, slot, sent.at[kind], sem, x_peer(i)).start()

    def tp_wait(buf, e, sem):
        arrived(buf.at[e, 0 : NX - 1], sem)

    def tp_sum(buf, e):
        total = buf[e, 0].astype(F32)
        for i in range(1, NX):
            total = total + buf[e, i].astype(F32)
        return total

    loads[0].wait()
    loads[2].wait()
    acc = jnp.zeros((T, HD), F32)
    for j in range(C // HD):
        piece = X[0, :, HD * j : HD * j + HD].astype(F32)
        acc = acc + piece * piece
    SS[0, x] = token_rows(acc)
    tp_send_all(2, SS, 0, tp_recv.at[5, 0])

    def spread(l, carry):
        slot = wbuf.at[l, c, y, z]
        arrived(slot, s1_recv.at[l])

        def go(i, inner):
            remote(slot, slot, sent.at[5], z_recv.at[l], z_peer((z + i) % NZ)).start()
            return inner

        return lax.fori_loop(1, NZ, go, carry)

    lax.fori_loop(0, L, spread, 0)

    def along_y(l):
        arrived(wbuf.at[l, c, y, 0 : NZ - 1], z_recv.at[l])
        slot = wbuf.at[l, c, y]
        for i in (1, 3):
            remote(slot, slot, sent.at[6], y_recv.at[l], y_peer((y + i) % NY)).start()

    def along_y_again(l):
        arrived(wbuf.at[l, c, 0:2], y_recv.at[l])
        for i, half in ((1, 0), (3, NZ // 2)):
            slot = wbuf.at[l, c, (y + NY - i) % NY, half : half + NZ // 2]
            remote(slot, slot, sent.at[12], y2_recv.at[l], y_peer((y + i) % NY)).start()

    def to_core(l):
        arrived(wbuf.at[l, c, 0], y2_recv.at[l])
        slot = wbuf.at[l, c]
        remote(slot, slot, sent.at[7], k_recv.at[l], core_peer).start()

    along_y(0)
    along_y(1)
    along_y_again(0)
    along_y(2)
    along_y_again(1)
    to_core(0)
    along_y(3)
    along_y_again(2)
    to_core(1)

    def w1(l, t):
        return jnp.concatenate(
            [
                wbuf[l, cc, yy, 2 * t + h, 0:16, :]
                for cc in range(2) for h in range(2) for yy in range(NY)
            ],
            axis=0,
        )

    def w2(l, t):
        heads = [
            jnp.concatenate(
                [wbuf[l, cc, yy, 2 * t + h, 16:32, :] for h in range(2) for yy in range(NY)], axis=0
            )
            for cc in range(2)
        ]
        return jnp.concatenate(heads, axis=1)

    def gains(l, t):
        heads = []
        for cc in range(2):
            g8 = wbuf[l, cc, 0, 2 * t, 32:40, :].astype(F32)
            heads.append(jnp.concatenate([g8] * 8, axis=0))
        return jnp.concatenate(heads, axis=1)

    def cols_of(t):
        return slice(256 * t, 256 * t + 256)

    def lanes_of(t):
        return slice(HD * t, HD * t + HD)

    def gram_part(l):
        total = jnp.zeros((HD, HD), F32)
        for t in range(4):
            block = w2(l, t)
            total = total + dot_nt(block, block)
        for i in range(NX):
            GP[l, i] = total[32 * i : 32 * i + 32]
        GX[l, x] = GP[l, x]
        for i in (2, 1, 3):
            dst = (x + i) % NX
            remote(
                GP.at[l, dst], GX.at[l, x], sent.at[13], tp_recv.at[3, l % 2], x_peer(i)
            ).start()

    def gram_sum(l):
        tp_wait(GX, l, tp_recv.at[3, l % 2])
        GF[l, x] = tp_sum(GX, l)
        tp_send_all(14, GF, l, tp_recv.at[4, l % 2])

    arrived(wbuf.at[0, c], k_recv.at[0])
    gram_part(0)

    def forward(l, carry):
        raw = []
        for t in range(4):
            h = (X[l, :, cols_of(t)].astype(F32) * gains(l, t)).astype(BF16)
            H[l, :, cols_of(t)] = h
            raw.append(dot_nt(h, pair_blocks(h)))

        @pl.when(l < L - 1)
        def _():
            u = jnp.zeros((T, HD), F32)
            for t in range(4):
                u = u + dot_nt(X[l, :, cols_of(t)], w2(l, t))
            UU[l, x] = u.astype(BF16)
            tp_send_all(3, UU, l, tp_recv.at[1, l % 2])

        @pl.when(l == 0)
        def _():
            tp_wait(SS, 0, tp_recv.at[5, 0])
            Q[...] = tp_sum(SS, 0)

        @pl.when(l > 0)
        def _():
            below = jnp.maximum(l - 1, 0)
            tp_wait(UU, below, tp_recv.at[1, below % 2])
            tp_wait(GF, below, tp_recv.at[4, below % 2])
            gram = GF[below].reshape(HD, HD)
            high = gram.astype(BF16)
            low = (gram - high.astype(F32)).astype(BF16)
            r = R[below]
            u = tp_sum(UU, below)
            rg = dot(jnp.concatenate((r, r), axis=1), jnp.concatenate((high, low), axis=0))
            BS[l] = u + rg
            Q[...] = Q[...] + token_rows(r.astype(F32) * (2.0 * u + rg))

        f_row = lax.rsqrt(jnp.maximum(Q[...], 0.0) * (1.0 / D) + 1e-05)
        Fr[l] = f_row
        f_key = f_row[0:1]
        scale = to_column(f_row) * f_key * (1.0 / HD)
        mask = MK[...]
        part = jnp.zeros((T, HD), F32)
        for t in range(4):
            e = jnp.exp(raw[t] * scale).astype(BF16)
            ES[l, :, lanes_of(t)] = e
            e = (e.astype(F32) * mask).astype(BF16)
            sums = dot(e, ones_wide)
            weighted = dot((e.astype(F32) * f_key).astype(BF16), pair_blocks(H[l, :, cols_of(t)]))
            mixed = (weighted / sums).astype(BF16)
            M[l, :, cols_of(t)] = mixed
            part = part + dot(mixed, w1(l, t))
        RR[l, x] = part.astype(BF16)
        tp_send_all(1, RR, l, tp_recv.at[0, l % 2])

        @pl.when(l == L - 1)
        def _():
            loads[1].wait()
            loads[3].wait()
            acc = jnp.zeros((T, HD), F32)
            for t in range(4):
                acc = acc + dot_nt(M[L, :, cols_of(t)], w2(L - 1, t))
            AA[L - 1, x, 0:64, :] = acc.astype(BF16)
            AA[L - 1, x, 64:80, :] = jnp.zeros((16, HD), BF16)
            tp_send_all(4, AA, L - 1, tp_recv.at[2, (L - 1) % 2])
            DYP[...] = M[L].astype(F32)

        @pl.when(l < L - 1)
        def _():
            gram_sum(l)

        @pl.when(l + 2 < L)
        def _():
            to_core(l + 2)

        @pl.when(l + 3 < L)
        def _():
            along_y_again(l + 3)

        @pl.when(l + 4 < L)
        def _():
            along_y(l + 4)

        @pl.when(l + 1 < L)
        def _():
            arrived(wbuf.at[l + 1, c], k_recv.at[l + 1])

        @pl.when(l + 1 < L - 1)
        def _():
            gram_part(l + 1)

        tp_wait(RR, l, tp_recv.at[0, l % 2])
        r = tp_sum(RR, l).astype(BF16)
        R[l] = r

        @pl.when(l < L - 1)
        def _():
            for t in range(4):
                X[l + 1, :, cols_of(t)] = (
                    X[l, :, cols_of(t)].astype(F32) + dot(r, w2(l, t))
                ).astype(BF16)

        return carry

    lax.fori_loop(0, L, forward, 0)

    def one_layer(l):
        f_row = Fr[l]
        f_key = f_row[0:1]
        f_col = to_column(f_row)
        mask = MK[...]
        mask_t = MKT[...]
        for t in range(4):
            es = ES[l, :, lanes_of(t)].astype(F32)
            e = es * mask
            sums = dot(e.astype(BF16), ones_blocks)
            PS[:, lanes_of(t)] = e / sums
            et = es * mask_t
            PT[:, lanes_of(t)] = et / jnp.sum(et, axis=0, keepdims=True)
            weight = w1(l, t)
            for src, dst in ((H, ZS), (M, YS)):
                pair = src[l, :, cols_of(t)]
                products = [
                    dot(pair[:, :HD], weight[:HD]), dot(pair[:, HD:], weight[HD:])
                ]
                dst[:, cols_of(t)] = jnp.concatenate(products, axis=1).astype(BF16)

        tp_wait(AA, l, tp_recv.at[2, l % 2])
        total = tp_sum(AA, l)
        s_row = total[64:72] + total[72:80]
        f_next = Fr[l + 1]
        coef = to_column(f_next * f_next * f_next * s_row * (1.0 / D))
        dr = total[:64] - coef * BS[l + 1]
        dr_b = dr.astype(BF16)
        dr_blocks = pair_blocks(twice(dr_b))
        dr2 = twice(dr)
        coef2 = twice(coef)
        f_col2 = twice(f_col)
        s_part = jnp.zeros((T, HD), F32)
        acc = jnp.zeros((T, HD), F32)
        below = jnp.maximum(l - 1, 0)
        for t in range(4):
            h = H[l, :, cols_of(t)]
            blocks = pair_blocks(h)
            dm = dot_nt(dr_b, w1(l, t)).astype(BF16)
            dm_blocks = pair_blocks(dm)
            prob = PS[:, lanes_of(t)]
            prob_t = PT[:, lanes_of(t)]
            zs = ZS[:, cols_of(t)]
            inner = dot((dr2 * YS[:, cols_of(t)].astype(F32)).astype(BF16), ones_heads)
            dp = dot_nt(dr_b, jnp.concatenate((zs[:, :HD], zs[:, HD:]), axis=0)) * f_key
            dp_t = dot_nt(zs, dr_blocks) * f_col
            ds = prob * (dp - inner)
            inner_t = jnp.sum(prob_t * dp_t, axis=0, keepdims=True)
            ds_t = prob_t * (dp_t - inner_t)
            both = (ds + ds_t) * f_key * (1.0 / HD)
            left = jnp.concatenate((both.astype(BF16), prob_t.astype(BF16)), axis=1)
            dn = dot(left, jnp.concatenate((blocks, dm_blocks), axis=0))
            xs = X[l, :, cols_of(t)].astype(F32)
            gdn = dn * gains(l, t)
            dy = DYP[:, cols_of(t)] - X[l + 1, :, cols_of(t)].astype(F32) * coef2
            M[L, :, cols_of(t)] = dy.astype(BF16)
            dyp = dy + gdn * f_col2
            DYP[:, cols_of(t)] = dyp
            acc = acc + dot_nt(dyp.astype(BF16), w2(below, t))
            prod = gdn * xs
            s_part = s_part + prod[:, :HD] + prod[:, HD:]
            dgain = jnp.sum(dn * xs * f_col2, axis=0, keepdims=True)
            wide = jnp.broadcast_to(dgain, (8, 256)).astype(BF16)
            for cc in range(2):
                for h2 in range(2):
                    for yy in range(NY):
                        G[l, cc, yy, 2 * t + h2, 32:40, :] = wide[:, HD * cc : HD * cc + HD]

        @pl.when(l > 0)
        def _():
            s_new = token_rows(s_part)
            s_high = s_new.astype(BF16).astype(F32)
            AA[below, x, 0:64, :] = acc.astype(BF16)
            AA[below, x, 64:80, :] = jnp.concatenate((s_high, s_new - s_high), axis=0).astype(BF16)
            tp_send_all(4, AA, below, tp_recv.at[2, below % 2])

        zeros = jnp.zeros((T, HD), F32)
        dr_t = jnp.transpose(jnp.concatenate((dr, zeros), axis=0)).astype(BF16)[:, :T]
        r_t = jnp.transpose(jnp.concatenate((R[l].astype(F32), zeros), axis=0)).astype(BF16)[:, :T]
        for t in range(4):
            g1 = dot(dr_t, M[l, :, cols_of(t)]).astype(BF16)
            g2 = dot(r_t, M[L, :, cols_of(t)]).astype(BF16)
            for cc in range(2):
                for q in range(8):
                    rows = slice(64 * (q % 2) + 16 * (q // 2), 64 * (q % 2) + 16 * (q // 2) + 16)
                    lanes = slice(HD * cc, HD * cc + HD)
                    G[l, cc, q // 2, 2 * t + q % 2, 0:16, :] = g1[rows, lanes]
                    G[l, cc, q // 2, 2 * t + q % 2, 16:32, :] = g2[rows, lanes]
        remote(G.at[l, 1 - c], RA.at[l], sent.at[8], ga_recv.at[l], core_peer).start()

    def core_sums(l):
        arrived(RA.at[l], ga_recv.at[l])

        def one(i, carry):
            SA[l, i] = (G[l, c, i].astype(F32) + RA[l, i].astype(F32)).astype(BF16)
            return carry

        lax.fori_loop(0, NY, one, 0)
        RB[l, y] = SA[l, y]
        for i in (2, 1, 3):
            yy = (y + i) % NY
            remote(SA.at[l, yy], RB.at[l, y], sent.at[9], gy_recv.at[l], y_peer(yy)).start()

    def y_sums(l):
        arrived(RB.at[l, 0 : NY - 1], gy_recv.at[l])
        total = RB[l, 0].astype(F32)
        for i in range(1, NY):
            total = total + RB[l, i].astype(F32)
        SB[l] = total.astype(BF16)
        RC[l, z] = SB[l, z]

        def go(i, carry):
            zz = (z + i) % NZ
            remote(SB.at[l, zz], RC.at[l, z], sent.at[10], gz_recv.at[l], z_peer(zz)).start()
            return carry

        lax.fori_loop(1, NZ, go, 0)

    def z_sums(l):
        arrived(RC.at[l, 0 : NZ - 1], gz_recv.at[l])
        total = RC[l, 0].astype(F32)
        for i in range(1, NZ):
            total = total + RC[l, i].astype(F32)
        SD[l] = total.astype(BF16)
        mine = is_me(owner(l))

        @pl.when(mine)
        def _():
            pltpu.make_async_copy(SD.at[l], RD.at[y, z % 2], go_recv.at[0]).start()

        @pl.when(jnp.logical_not(mine))
        def _():
            remote(SD.at[l], RD.at[y, z % 2], sent.at[11], go_recv.at[0], owner(l)).start()

    def backward(i, carry):
        @pl.when(i < L)
        def _():
            one_layer(L - 1 - i)

        @pl.when((i >= 1) & (i < L + 1))
        def _():
            core_sums(L - i)

        @pl.when((i >= 3) & (i < L + 3))
        def _():
            y_sums(L + 2 - i)

        @pl.when(i >= 4)
        def _():
            z_sums(L + 3 - i)

        return carry

    lax.fori_loop(0, L + 4, backward, 0)

    arrived(RD, go_recv.at[0])
    grads = []
    for part in range(2):
        rows = slice(16 * part, 16 * part + 16)
        blocks = [RD[yy, h, rows, :].astype(F32) for h in range(2) for yy in range(NY)]
        grads.append(jnp.concatenate(blocks, axis=0))
    first_out[0] = jnp.transpose(grads[0])
    second_out[0] = grads[1]
    gain_out[...] = RD[0, 0, 32:40, :].astype(F32)[0:1]

    for used, sem, pieces in ((me_holder, 0, chunk), (me_owner, 11, SD)):
        @pl.when(used > 0)
        def _():
            arrived(pieces.at[0:7], sent.at[sem])

        @pl.when(used == 0)
        def _():
            arrived(pieces, sent.at[sem])

    arrived(RR.at[0:6], sent.at[1])
    arrived(SS.at[0, 0:3], sent.at[2])
    arrived(UU.at[0:7, 0:3], sent.at[3])
    arrived(AA.at[0:6], sent.at[4])
    arrived(wbuf.at[0:7, 0, 0], sent.at[5])
    arrived(wbuf.at[0:2], sent.at[6])
    arrived(wbuf.at[0:1], sent.at[12])
    arrived(GP.at[0:7, 0:3], sent.at[13])
    arrived(GF.at[0:7, 0:3], sent.at[14])
    arrived(wbuf.at[0:4], sent.at[7])
    arrived(G.at[0:4], sent.at[8])
    arrived(SA.at[0:6], sent.at[9])
    arrived(SB.at[0:7], sent.at[10])


def per_device(tokens, cotangents, starts, counts, layer_gains, first_map, second_map):
    vmem = pl.BlockSpec(memory_space=pltpu.VMEM)
    smem = pl.BlockSpec(memory_space=pltpu.SMEM)
    hbm = pl.BlockSpec(memory_space=pltpu.HBM)
    sem = pltpu.SemaphoreType.DMA
    return pl.pallas_call(
        kernel,
        out_shape=(
            jax.ShapeDtypeStruct((1, HD), F32),
            jax.ShapeDtypeStruct((1, HD, HD), F32),
            jax.ShapeDtypeStruct((1, HD, HD), F32),
        ),
        in_specs=[hbm, hbm, smem, smem, hbm, hbm, hbm],
        out_specs=(vmem, vmem, vmem),
        scratch_shapes=[
            pltpu.VMEM((8, PR, HD), BF16),
            pltpu.VMEM((1, HD), BF16),
            pltpu.VMEM((1, HD, HD), BF16),
            pltpu.VMEM((1, HD, HD), BF16),
            pltpu.VMEM((L, 2, NY, NZ, PR, HD), BF16),
            pltpu.VMEM((L + 1, T, C), BF16),
            pltpu.VMEM((L, T, C), BF16),
            pltpu.VMEM((L + 1, T, C), BF16),
            pltpu.VMEM((L, T, 4 * HD), BF16),
            pltpu.VMEM((L + 1, 8, HD), F32),
            pltpu.VMEM((L, T, HD), BF16),
            pltpu.VMEM((L, NX, T, HD), BF16),
            pltpu.VMEM((1, NX, 8, HD), F32),
            pltpu.VMEM((L, NX, T, HD), BF16),
            pltpu.VMEM((L, NX, 80, HD), BF16),
            pltpu.VMEM((L + 1, T, HD), F32),
            pltpu.VMEM((8, HD), F32),
            pltpu.VMEM((L, NX, HD // NX, HD), F32),
            pltpu.VMEM((L, NX, HD // NX, HD), F32),
            pltpu.VMEM((L, NX, HD // NX, HD), F32),
            pltpu.VMEM((T, 4 * HD), F32),
            pltpu.VMEM((T, 4 * HD), F32),
            pltpu.VMEM((T, C), BF16),
            pltpu.VMEM((T, C), BF16),
            pltpu.VMEM((T, C), F32),
            pltpu.VMEM((T, HD), F32),
            pltpu.VMEM((T, HD), F32),
            pltpu.VMEM((L, 2, NY, NZ, PR, HD), BF16),
            pltpu.VMEM((L, NY, NZ, PR, HD), BF16),
            pltpu.VMEM((L, NY, NZ, PR, HD), BF16),
            pltpu.VMEM((L, NY, NZ, PR, HD), BF16),
            pltpu.VMEM((L, NZ, PR, HD), BF16),
            pltpu.VMEM((L, NZ, PR, HD), BF16),
            pltpu.VMEM((L, PR, HD), BF16),
            pltpu.VMEM((NY, 2, PR, HD), BF16),
            sem((7,)), sem((15,)),
            sem((L,)), sem((L,)), sem((L,)), sem((L,)), sem((L,)),
            sem((6, 2)),
            sem((L,)), sem((L,)), sem((L,)), sem((1,)),
        ],
        compiler_params=pltpu.CompilerParams(
            collective_id=0, has_side_effects=True, vmem_limit_bytes=VMEM_LIMIT
        ),
    )(tokens, cotangents, starts, counts, layer_gains, first_map, second_map)


def solution(mesh):
    in_specs = (
        P(None, "dp", None, None),
        P(None, "dp", None, None),
        P(None, "dp", None),
        P(None, "dp"),
        P("pipe", "dp"),
        P("pipe", "dp", None),
        P("pipe", None, "dp"),
    )
    out_specs = (P("pipe", "dp"), P("pipe", "dp", None), P("pipe", None, "dp"))
    return jax.shard_map(
        per_device, mesh=mesh, in_specs=in_specs, out_specs=out_specs, check_vma=False
    )
```

```python
import jax
import jax.numpy as jnp
from jax import lax
from jax.experimental import pallas as pl
from jax.experimental.pallas import tpu as pltpu
from jax.sharding import PartitionSpec as P

MESH = pl.DeviceIdType.MESH
F32 = jnp.float32
BF16 = jnp.bfloat16
L = 8
NX = 4
NZ = 8
NY = 4
HD = 128
T = 64
C = 1024
PR = 40
D = 4096
VMEM_LIMIT = 67043328 - 136 * 1024


def dot(a, b):
    return lax.dot_general(a, b, (((1,), (0,)), ((), ())), preferred_element_type=F32)


def dot_nt(a, b):
    return lax.dot_general(a, b, (((1,), (1,)), ((), ())), preferred_element_type=F32)


def pair_blocks(v):
    zero = jnp.zeros((T, HD), v.dtype)
    top = jnp.concatenate((v[:, :HD], zero), axis=1)
    low = jnp.concatenate((zero, v[:, HD:]), axis=1)
    return jnp.concatenate((top, low), axis=0)


def token_rows(p):
    both = jnp.concatenate((p, p), axis=0)
    high = both.astype(BF16)
    low = (both - high.astype(F32)).astype(BF16)
    return dot_nt(jnp.ones((16, 2 * HD), BF16), jnp.concatenate((high, low), axis=1))[:8]


def to_column(row):
    return jnp.transpose(jnp.broadcast_to(row[0:1], (HD, HD)))[:T]


def twice(v):
    return jnp.concatenate((v, v), axis=1)


def kernel(
    tok, cot, starts, counts, gain_in, first_in, second_in,
    gain_out, first_out, second_out,
    chunk, own_gain, own_first, own_second, wbuf, X, H, M, ES, Fr, R, RR, SS, UU, AA, BS, Q, GP, GX, GF,
    PS, PT, ZS, YS, DYP, MK, MKT, G, RA, SA, RB, SB, RC, SD, RD,
    in_sem, sent, s1_recv, z_recv, y_recv, y2_recv, k_recv, tp_recv,
    ga_recv, gy_recv, gz_recv, go_recv,
):
    p = lax.axis_index("pipe")
    d = lax.axis_index("dp")
    x, yh = p // 2, p % 2
    yl, z, c = d // 16, (d // 2) % 8, d % 2
    y = 2 * yh + yl
    k_own = z % 4

    def x_peer(i):
        return (((x + i) % NX) * 2 + yh, d)

    def z_peer(zz):
        return (p, yl * 16 + zz * 2 + c)

    def y_peer(yy):
        return (x * 2 + yy // 2, (yy % 2) * 16 + z * 2 + c)

    core_peer = (p, d + 1 - 2 * c)

    def holder(q):
        yy, h = q // 2, q % 2
        return ((d // 8) * 2 + yy // 2, (yy % 2) * 16 + (2 * k_own + h) * 2 + c)

    def owner(l):
        return (l, 8 * x + 2 * (z // 2) + c)

    def is_me(dev):
        return (dev[0] == p) & (dev[1] == d)

    def arrived(ref, sem):
        pltpu.make_async_copy(ref, ref, sem).wait()

    def remote(src, dst, ss, rs, dev):
        return pltpu.make_async_remote_copy(
            src_ref=src, dst_ref=dst, send_sem=ss, recv_sem=rs, device_id=dev, device_id_type=MESH
        )

    cols = pl.ds(pl.multiple_of(x * C, C), C)
    loads = []
    for b in range(2):
        rows = pl.ds(32 * b, 32)
        loads.append(pltpu.make_async_copy(tok.at[yh, b, :, cols], X.at[0, rows, :], in_sem.at[b]))
        loads.append(pltpu.make_async_copy(cot.at[yh, b, :, cols], M.at[L, rows, :], in_sem.at[2 + b]))
    chunk_loads = [
        pltpu.make_async_copy(first_in, own_first, in_sem.at[4]),
        pltpu.make_async_copy(second_in, own_second, in_sem.at[5]),
        pltpu.make_async_copy(gain_in, own_gain, in_sem.at[6]),
    ]
    for load in chunk_loads + loads:
        load.start()

    barrier = pltpu.get_barrier_semaphore()

    def greet(dev):
        pl.semaphore_signal(barrier, inc=1, device_id=dev, device_id_type=MESH)

    def greet_x(i, carry):
        greet(x_peer(i))
        return carry

    def greet_z(i, carry):
        greet(z_peer((z + i) % NZ))
        return carry

    def greet_y(i, carry):
        greet(y_peer((y + i) % NY))
        return carry

    def greet_far(q, carry):
        for dev in (holder(q), owner(q)):
            @pl.when(jnp.logical_not(is_me(dev)))
            def _():
                greet(dev)
        return carry

    lax.fori_loop(0, 8, greet_far, 0)
    lax.fori_loop(1, NZ, greet_z, 0)
    lax.fori_loop(1, NY, greet_y, 0)
    lax.fori_loop(1, NX, greet_x, 0)
    greet(core_peer)

    row_id = lax.broadcasted_iota(jnp.int32, (T, HD), 0)
    lane_id = lax.broadcasted_iota(jnp.int32, (T, HD), 1) % T

    def documents(index):
        second_mb = index >= 32
        pos = jnp.where(second_mb, index - 32, index)
        doc = jnp.zeros((T, HD), jnp.int32)
        count = jnp.where(second_mb, counts[yh, 1], counts[yh, 0])
        for j in range(4):
            start = jnp.where(second_mb, starts[yh, 1, j], starts[yh, 0, j])
            doc = doc + jnp.where((start <= pos) & (j < count), 1, 0)
        return doc + jnp.where(second_mb, 64, 0)

    same = documents(row_id) == documents(lane_id)
    MK[...] = jnp.where(same & (lane_id <= row_id), 1.0, 0.0)
    MKT[...] = jnp.where(same & (row_id <= lane_id), 1.0, 0.0)
    Fr[L] = jnp.zeros((8, HD), F32)
    BS[L] = jnp.zeros((T, HD), F32)
    X[L] = jnp.zeros((T, C), BF16)
    half_r = lax.broadcasted_iota(jnp.int32, (HD, HD), 0) // T
    half_l = lax.broadcasted_iota(jnp.int32, (HD, HD), 1) // T
    ones_blocks = jnp.where(half_r == half_l, 1.0, 0.0).astype(BF16)
    wide_r = lax.broadcasted_iota(jnp.int32, (HD, 2 * HD), 0) // T
    wide_l = lax.broadcasted_iota(jnp.int32, (HD, 2 * HD), 1) // HD
    ones_wide = jnp.where(wide_r == wide_l, 1.0, 0.0).astype(BF16)
    head_r = lax.broadcasted_iota(jnp.int32, (2 * HD, HD), 0) // HD
    head_l = lax.broadcasted_iota(jnp.int32, (2 * HD, HD), 1) // T
    ones_heads = jnp.where(head_r == head_l, 1.0, 0.0).astype(BF16)

    me_holder = jnp.int32(0)
    me_owner = jnp.int32(0)
    for q in range(8):
        me_holder = me_holder + jnp.where(is_me(holder(q)), 1, 0)
        me_owner = me_owner + jnp.where(is_me(owner(q)), 1, 0)
    for load in chunk_loads:
        load.wait()
    for q in range(8):
        rows = slice(64 * (q % 2) + 16 * (q // 2), 64 * (q % 2) + 16 * (q // 2) + 16)
        chunk[q, 0:16, :] = own_first[0, rows, :]
        chunk[q, 16:32, :] = own_second[0, rows, :]
        chunk[q, 32:40, :] = jnp.broadcast_to(own_gain[0:1, :].astype(F32), (8, HD)).astype(BF16)
    pl.semaphore_wait(barrier, 30 - me_holder - me_owner)

    def s1_start(q, carry):
        mine = is_me(holder(q))
        slot = wbuf.at[p, c, q // 2, 2 * k_own + q % 2]

        @pl.when(mine)
        def _():
            pltpu.make_async_copy(chunk.at[q], slot, s1_recv.at[p]).start()

        @pl.when(jnp.logical_not(mine))
        def _():
            remote(chunk.at[q], slot, sent.at[0], s1_recv.at[p], holder(q)).start()

        return carry

    lax.fori_loop(0, 8, s1_start, 0)

    def tp_send_all(kind, buf, e, sem):
        slot = buf.at[e, x]
        for i in (2, 1, 3):
            remote(slot, slot, sent.at[kind], sem, x_peer(i)).start()

    def tp_wait(buf, e, sem):
        arrived(buf.at[e, 0 : NX - 1], sem)

    def tp_sum(buf, e):
        total = buf[e, 0].astype(F32)
        for i in range(1, NX):
            total = total + buf[e, i].astype(F32)
        return total

    loads[0].wait()
    loads[2].wait()
    acc = jnp.zeros((T, HD), F32)
    for j in range(C // HD):
        piece = X[0, :, HD * j : HD * j + HD].astype(F32)
        acc = acc + piece * piece
    SS[0, x] = token_rows(acc)
    tp_send_all(2, SS, 0, tp_recv.at[5, 0])

    def spread(l, carry):
        slot = wbuf.at[l, c, y, z]
        arrived(slot, s1_recv.at[l])

        def go(i, inner):
            remote(slot, slot, sent.at[5], z_recv.at[l], z_peer((z + i) % NZ)).start()
            return inner

        return lax.fori_loop(1, NZ, go, carry)

    lax.fori_loop(0, L, spread, 0)

    def along_y(l):
        arrived(wbuf.at[l, c, y, 0 : NZ - 1], z_recv.at[l])
        slot = wbuf.at[l, c, y]
        for i in (1, 3):
            remote(slot, slot, sent.at[6], y_recv.at[l], y_peer((y + i) % NY)).start()

    def along_y_again(l):
        arrived(wbuf.at[l, c, 0:2], y_recv.at[l])
        for i, half in ((1, 0), (3, NZ // 2)):
            slot = wbuf.at[l, c, (y + NY - i) % NY, half : half + NZ // 2]
            remote(slot, slot, sent.at[12], y2_recv.at[l], y_peer((y + i) % NY)).start()

    def to_core(l):
        arrived(wbuf.at[l, c, 0], y2_recv.at[l])
        slot = wbuf.at[l, c]
        remote(slot, slot, sent.at[7], k_recv.at[l], core_peer).start()

    along_y(0)
    along_y(1)
    along_y_again(0)
    along_y(2)
    along_y_again(1)
    to_core(0)
    along_y(3)
    along_y_again(2)
    to_core(1)

    def w1(l, t):
        return jnp.concatenate(
            [
                wbuf[l, cc, yy, 2 * t + h, 0:16, :]
                for cc in range(2) for h in range(2) for yy in range(NY)
            ],
            axis=0,
        )

    def w2(l, t):
        heads = [
            jnp.concatenate(
                [wbuf[l, cc, yy, 2 * t + h, 16:32, :] for h in range(2) for yy in range(NY)], axis=0
            )
            for cc in range(2)
        ]
        return jnp.concatenate(heads, axis=1)

    def gains(l, t):
        heads = []
        for cc in range(2):
            g8 = wbuf[l, cc, 0, 2 * t, 32:40, :].astype(F32)
            heads.append(jnp.concatenate([g8] * 8, axis=0))
        return jnp.concatenate(heads, axis=1)

    def cols_of(t):
        return slice(256 * t, 256 * t + 256)

    def lanes_of(t):
        return slice(HD * t, HD * t + HD)

    def gram_part(l):
        total = jnp.zeros((HD, HD), F32)
        for t in range(4):
            block = w2(l, t)
            total = total + dot_nt(block, block)
        for i in range(NX):
            GP[l, i] = total[32 * i : 32 * i + 32]
        GX[l, x] = GP[l, x]
        for i in (2, 1, 3):
            dst = (x + i) % NX
            remote(
                GP.at[l, dst], GX.at[l, x], sent.at[13], tp_recv.at[3, l % 2], x_peer(i)
            ).start()

    def gram_sum(l):
        tp_wait(GX, l, tp_recv.at[3, l % 2])
        GF[l, x] = tp_sum(GX, l)
        tp_send_all(14, GF, l, tp_recv.at[4, l % 2])

    arrived(wbuf.at[0, c], k_recv.at[0])
    gram_part(0)

    def forward(l, carry):
        raw = []
        for t in range(4):
            h = (X[l, :, cols_of(t)].astype(F32) * gains(l, t)).astype(BF16)
            H[l, :, cols_of(t)] = h
            raw.append(dot_nt(h, pair_blocks(h)))

        @pl.when(l < L - 1)
        def _():
            u = jnp.zeros((T, HD), F32)
            for t in range(4):
                u = u + dot_nt(X[l, :, cols_of(t)], w2(l, t))
            UU[l, x] = u.astype(BF16)
            tp_send_all(3, UU, l, tp_recv.at[1, l % 2])

        @pl.when(l == 0)
        def _():
            tp_wait(SS, 0, tp_recv.at[5, 0])
            Q[...] = tp_sum(SS, 0)

        @pl.when(l > 0)
        def _():
            below = jnp.maximum(l - 1, 0)
            tp_wait(UU, below, tp_recv.at[1, below % 2])
            tp_wait(GF, below, tp_recv.at[4, below % 2])
            gram = GF[below].reshape(HD, HD)
            high = gram.astype(BF16)
            low = (gram - high.astype(F32)).astype(BF16)
            r = R[below]
            u = tp_sum(UU, below)
            rg = dot(jnp.concatenate((r, r), axis=1), jnp.concatenate((high, low), axis=0))
            BS[l] = u + rg
            Q[...] = Q[...] + token_rows(r.astype(F32) * (2.0 * u + rg))

        f_row = lax.rsqrt(jnp.maximum(Q[...], 0.0) * (1.0 / D) + 1e-05)
        Fr[l] = f_row
        f_key = f_row[0:1]
        scale = to_column(f_row) * f_key * (1.0 / HD)
        mask = MK[...]
        part = jnp.zeros((T, HD), F32)
        for t in range(4):
            e = jnp.exp(raw[t] * scale).astype(BF16)
            ES[l, :, lanes_of(t)] = e
            e = (e.astype(F32) * mask).astype(BF16)
            sums = dot(e, ones_wide)
            weighted = dot((e.astype(F32) * f_key).astype(BF16), pair_blocks(H[l, :, cols_of(t)]))
            mixed = (weighted / sums).astype(BF16)
            M[l, :, cols_of(t)] = mixed
            part = part + dot(mixed, w1(l, t))
        RR[l, x] = part.astype(BF16)
        tp_send_all(1, RR, l, tp_recv.at[0, l % 2])

        @pl.when(l == L - 1)
        def _():
            loads[1].wait()
            loads[3].wait()
            acc = jnp.zeros((T, HD), F32)
            for t in range(4):
                acc = acc + dot_nt(M[L, :, cols_of(t)], w2(L - 1, t))
            AA[L - 1, x, 0:64, :] = acc.astype(BF16)
            AA[L - 1, x, 64:72, :] = jnp.zeros((8, HD), BF16)
            tp_send_all(4, AA, L - 1, tp_recv.at[2, (L - 1) % 2])
            DYP[...] = M[L].astype(F32)

        @pl.when(l < L - 1)
        def _():
            gram_sum(l)

        @pl.when(l + 2 < L)
        def _():
            to_core(l + 2)

        @pl.when(l + 3 < L)
        def _():
            along_y_again(l + 3)

        @pl.when(l + 4 < L)
        def _():
            along_y(l + 4)

        @pl.when(l + 1 < L)
        def _():
            arrived(wbuf.at[l + 1, c], k_recv.at[l + 1])

        @pl.when(l + 1 < L - 1)
        def _():
            gram_part(l + 1)

        tp_wait(RR, l, tp_recv.at[0, l % 2])
        r = tp_sum(RR, l).astype(BF16)
        R[l] = r

        @pl.when(l < L - 1)
        def _():
            for t in range(4):
                X[l + 1, :, cols_of(t)] = (
                    X[l, :, cols_of(t)].astype(F32) + dot(r, w2(l, t))
                ).astype(BF16)

        return carry

    lax.fori_loop(0, L, forward, 0)

    def one_layer(l):
        f_row = Fr[l]
        f_key = f_row[0:1]
        f_col = to_column(f_row)
        mask = MK[...]
        mask_t = MKT[...]
        for t in range(4):
            es = ES[l, :, lanes_of(t)].astype(F32)
            e = es * mask
            sums = dot(e.astype(BF16), ones_blocks)
            PS[:, lanes_of(t)] = e / sums
            et = es * mask_t
            PT[:, lanes_of(t)] = et / jnp.sum(et, axis=0, keepdims=True)
            weight = w1(l, t)
            for src, dst in ((H, ZS), (M, YS)):
                pair = src[l, :, cols_of(t)]
                products = [
                    dot(pair[:, :HD], weight[:HD]), dot(pair[:, HD:], weight[HD:])
                ]
                dst[:, cols_of(t)] = jnp.concatenate(products, axis=1).astype(BF16)

        tp_wait(AA, l, tp_recv.at[2, l % 2])
        total = tp_sum(AA, l)
        s_row = total[64:72]
        f_next = Fr[l + 1]
        coef = to_column(f_next * f_next * f_next * s_row * (1.0 / D))
        dr = total[:64] - coef * BS[l + 1]
        dr_b = dr.astype(BF16)
        dr_blocks = pair_blocks(twice(dr_b))
        dr2 = twice(dr)
        coef2 = twice(coef)
        f_col2 = twice(f_col)
        s_part = jnp.zeros((T, HD), F32)
        acc = jnp.zeros((T, HD), F32)
        below = jnp.maximum(l - 1, 0)
        for t in range(4):
            h = H[l, :, cols_of(t)]
            blocks = pair_blocks(h)
            dm = dot_nt(dr_b, w1(l, t)).astype(BF16)
            dm_blocks = pair_blocks(dm)
            prob = PS[:, lanes_of(t)]
            prob_t = PT[:, lanes_of(t)]
            zs = ZS[:, cols_of(t)]
            inner = dot((dr2 * YS[:, cols_of(t)].astype(F32)).astype(BF16), ones_heads)
            dp = dot_nt(dr_b, jnp.concatenate((zs[:, :HD], zs[:, HD:]), axis=0)) * f_key
            dp_t = dot_nt(zs, dr_blocks) * f_col
            ds = prob * (dp - inner)
            inner_t = jnp.sum(prob_t * dp_t, axis=0, keepdims=True)
            ds_t = prob_t * (dp_t - inner_t)
            both = (ds + ds_t) * f_key * (1.0 / HD)
            left = jnp.concatenate((both.astype(BF16), prob_t.astype(BF16)), axis=1)
            dn = dot(left, jnp.concatenate((blocks, dm_blocks), axis=0))
            xs = X[l, :, cols_of(t)].astype(F32)
            gdn = dn * gains(l, t)
            dy = DYP[:, cols_of(t)] - X[l + 1, :, cols_of(t)].astype(F32) * coef2
            M[L, :, cols_of(t)] = dy.astype(BF16)
            dyp = dy + gdn * f_col2
            DYP[:, cols_of(t)] = dyp
            acc = acc + dot_nt(dyp.astype(BF16), w2(below, t))
            prod = gdn * xs
            s_part = s_part + prod[:, :HD] + prod[:, HD:]
            dgain = jnp.sum(dn * xs * f_col2, axis=0, keepdims=True)
            wide = jnp.broadcast_to(dgain, (8, 256)).astype(BF16)
            for cc in range(2):
                for h2 in range(2):
                    for yy in range(NY):
                        G[l, cc, yy, 2 * t + h2, 32:40, :] = wide[:, HD * cc : HD * cc + HD]

        @pl.when(l > 0)
        def _():
            s_new = token_rows(s_part)
            AA[below, x, 0:64, :] = acc.astype(BF16)
            AA[below, x, 64:72, :] = s_new.astype(BF16)
            tp_send_all(4, AA, below, tp_recv.at[2, below % 2])

        zeros = jnp.zeros((T, HD), F32)
        dr_t = jnp.transpose(jnp.concatenate((dr, zeros), axis=0)).astype(BF16)[:, :T]
        r_t = jnp.transpose(jnp.concatenate((R[l].astype(F32), zeros), axis=0)).astype(BF16)[:, :T]
        for t in range(4):
            g1 = dot(dr_t, M[l, :, cols_of(t)]).astype(BF16)
            g2 = dot(r_t, M[L, :, cols_of(t)]).astype(BF16)
            for cc in range(2):
                for q in range(8):
                    rows = slice(64 * (q % 2) + 16 * (q // 2), 64 * (q % 2) + 16 * (q // 2) + 16)
                    lanes = slice(HD * cc, HD * cc + HD)
                    G[l, cc, q // 2, 2 * t + q % 2, 0:16, :] = g1[rows, lanes]
                    G[l, cc, q // 2, 2 * t + q % 2, 16:32, :] = g2[rows, lanes]
        remote(G.at[l, 1 - c], RA.at[l], sent.at[8], ga_recv.at[l], core_peer).start()

    def core_sums(l):
        arrived(RA.at[l], ga_recv.at[l])

        def one(i, carry):
            SA[l, i] = (G[l, c, i].astype(F32) + RA[l, i].astype(F32)).astype(BF16)
            return carry

        lax.fori_loop(0, NY, one, 0)
        RB[l, y] = SA[l, y]
        for i in (2, 1, 3):
            yy = (y + i) % NY
            remote(SA.at[l, yy], RB.at[l, y], sent.at[9], gy_recv.at[l], y_peer(yy)).start()

    def y_sums(l):
        arrived(RB.at[l, 0 : NY - 1], gy_recv.at[l])
        total = RB[l, 0].astype(F32)
        for i in range(1, NY):
            total = total + RB[l, i].astype(F32)
        SB[l] = total.astype(BF16)
        RC[l, z] = SB[l, z]

        def go(i, carry):
            zz = (z + i) % NZ
            remote(SB.at[l, zz], RC.at[l, z], sent.at[10], gz_recv.at[l], z_peer(zz)).start()
            return carry

        lax.fori_loop(1, NZ, go, 0)

    def z_sums(l):
        arrived(RC.at[l, 0 : NZ - 1], gz_recv.at[l])
        total = RC[l, 0].astype(F32)
        for i in range(1, NZ):
            total = total + RC[l, i].astype(F32)
        SD[l] = total.astype(BF16)
        mine = is_me(owner(l))

        @pl.when(mine)
        def _():
            pltpu.make_async_copy(SD.at[l], RD.at[y, z % 2], go_recv.at[0]).start()

        @pl.when(jnp.logical_not(mine))
        def _():
            remote(SD.at[l], RD.at[y, z % 2], sent.at[11], go_recv.at[0], owner(l)).start()

    def backward(i, carry):
        @pl.when(i < L)
        def _():
            one_layer(L - 1 - i)

        @pl.when((i >= 1) & (i < L + 1))
        def _():
            core_sums(L - i)

        @pl.when((i >= 3) & (i < L + 3))
        def _():
            y_sums(L + 2 - i)

        @pl.when(i >= 4)
        def _():
            z_sums(L + 3 - i)

        return carry

    lax.fori_loop(0, L + 4, backward, 0)

    arrived(RD, go_recv.at[0])
    grads = []
    for part in range(2):
        rows = slice(16 * part, 16 * part + 16)
        blocks = [RD[yy, h, rows, :].astype(F32) for h in range(2) for yy in range(NY)]
        grads.append(jnp.concatenate(blocks, axis=0))
    first_out[0] = jnp.transpose(grads[0])
    second_out[0] = grads[1]
    gain_out[...] = RD[0, 0, 32:40, :].astype(F32)[0:1]

    for used, sem, pieces in ((me_holder, 0, chunk), (me_owner, 11, SD)):
        @pl.when(used > 0)
        def _():
            arrived(pieces.at[0:7], sent.at[sem])

        @pl.when(used == 0)
        def _():
            arrived(pieces, sent.at[sem])

    arrived(RR.at[0:6], sent.at[1])
    arrived(SS.at[0, 0:3], sent.at[2])
    arrived(UU.at[0:7, 0:3], sent.at[3])
    arrived(AA.at[0:6], sent.at[4])
    arrived(wbuf.at[0:7, 0, 0], sent.at[5])
    arrived(wbuf.at[0:2], sent.at[6])
    arrived(wbuf.at[0:1], sent.at[12])
    arrived(GP.at[0:7, 0:3], sent.at[13])
    arrived(GF.at[0:7, 0:3], sent.at[14])
    arrived(wbuf.at[0:4], sent.at[7])
    arrived(G.at[0:4], sent.at[8])
    arrived(SA.at[0:6], sent.at[9])
    arrived(SB.at[0:7], sent.at[10])


def per_device(tokens, cotangents, starts, counts, layer_gains, first_map, second_map):
    vmem = pl.BlockSpec(memory_space=pltpu.VMEM)
    smem = pl.BlockSpec(memory_space=pltpu.SMEM)
    hbm = pl.BlockSpec(memory_space=pltpu.HBM)
    sem = pltpu.SemaphoreType.DMA
    return pl.pallas_call(
        kernel,
        out_shape=(
            jax.ShapeDtypeStruct((1, HD), F32),
            jax.ShapeDtypeStruct((1, HD, HD), F32),
            jax.ShapeDtypeStruct((1, HD, HD), F32),
        ),
        in_specs=[hbm, hbm, smem, smem, hbm, hbm, hbm],
        out_specs=(vmem, vmem, vmem),
        scratch_shapes=[
            pltpu.VMEM((8, PR, HD), BF16),
            pltpu.VMEM((1, HD), BF16),
            pltpu.VMEM((1, HD, HD), BF16),
            pltpu.VMEM((1, HD, HD), BF16),
            pltpu.VMEM((L, 2, NY, NZ, PR, HD), BF16),
            pltpu.VMEM((L + 1, T, C), BF16),
            pltpu.VMEM((L, T, C), BF16),
            pltpu.VMEM((L + 1, T, C), BF16),
            pltpu.VMEM((L, T, 4 * HD), BF16),
            pltpu.VMEM((L + 1, 8, HD), F32),
            pltpu.VMEM((L, T, HD), BF16),
            pltpu.VMEM((L, NX, T, HD), BF16),
            pltpu.VMEM((1, NX, 8, HD), F32),
            pltpu.VMEM((L, NX, T, HD), BF16),
            pltpu.VMEM((L, NX, 72, HD), BF16),
            pltpu.VMEM((L + 1, T, HD), F32),
            pltpu.VMEM((8, HD), F32),
            pltpu.VMEM((L, NX, HD // NX, HD), F32),
            pltpu.VMEM((L, NX, HD // NX, HD), F32),
            pltpu.VMEM((L, NX, HD // NX, HD), F32),
            pltpu.VMEM((T, 4 * HD), F32),
            pltpu.VMEM((T, 4 * HD), F32),
            pltpu.VMEM((T, C), BF16),
            pltpu.VMEM((T, C), BF16),
            pltpu.VMEM((T, C), F32),
            pltpu.VMEM((T, HD), F32),
            pltpu.VMEM((T, HD), F32),
            pltpu.VMEM((L, 2, NY, NZ, PR, HD), BF16),
            pltpu.VMEM((L, NY, NZ, PR, HD), BF16),
            pltpu.VMEM((L, NY, NZ, PR, HD), BF16),
            pltpu.VMEM((L, NY, NZ, PR, HD), BF16),
            pltpu.VMEM((L, NZ, PR, HD), BF16),
            pltpu.VMEM((L, NZ, PR, HD), BF16),
            pltpu.VMEM((L, PR, HD), BF16),
            pltpu.VMEM((NY, 2, PR, HD), BF16),
            sem((7,)), sem((15,)),
            sem((L,)), sem((L,)), sem((L,)), sem((L,)), sem((L,)),
            sem((6, 2)),
            sem((L,)), sem((L,)), sem((L,)), sem((1,)),
        ],
        compiler_params=pltpu.CompilerParams(
            collective_id=0, has_side_effects=True, vmem_limit_bytes=VMEM_LIMIT
        ),
    )(tokens, cotangents, starts, counts, layer_gains, first_map, second_map)


def solution(mesh):
    in_specs = (
        P(None, "dp", None, None),
        P(None, "dp", None, None),
        P(None, "dp", None),
        P(None, "dp"),
        P("pipe", "dp"),
        P("pipe", "dp", None),
        P("pipe", None, "dp"),
    )
    out_specs = (P("pipe", "dp"), P("pipe", "dp", None), P("pipe", None, "dp"))
    return jax.shard_map(
        per_device, mesh=mesh, in_specs=in_specs, out_specs=out_specs, check_vma=False
    )
```
